32 devices in a mesh: dp: 4 (over y, x), seq: 8 (over z, core).
Axes of the slice: x: 2, y: 2, z: 4, core: 2. Of those that a mesh axis runs over, the one named last changes fastest.
Arguments:
- block_input: bfloat16 [4, 1536, 2560], P('dp', 'seq'), may hold values from -70 to 70
- qkv_weight: bfloat16 [2560, 1792], P(('dp', 'seq')), may hold values from -1 to 1
- out_weight: bfloat16 [2560, 1280], P(('dp', 'seq')), may hold values from -6 to 6
- ffn_weight: bfloat16 [2560, 7680], P(('dp', 'seq')), may hold values from -0.125 to 0.125
- down_weight: bfloat16 [2560, 3840], P(('dp', 'seq')), may hold values from -0.09375 to 0.09375
- attn_gain: bfloat16 [2560], P(('dp', 'seq')), may hold values from 0.099609375 to 1.8984375
- ffn_gain: bfloat16 [2560], P(('dp', 'seq')), may hold values from 0.099609375 to 1.8984375
- cotangent: bfloat16 [4, 1536, 2560], P('dp', 'seq'), may hold values from -6 to 6
Outputs:
- block_output: bfloat16 [4, 1536, 2560], P('dp', 'seq')
- grad_input: float32 [4, 1536, 2560], P('dp', 'seq')
- grad_qkv: float32 [2560, 1792], P(('dp', 'seq'))
- grad_out: float32 [2560, 1280], P(('dp', 'seq'))
- grad_ffn: float32 [2560, 7680], P(('dp', 'seq'))
- grad_down: float32 [2560, 3840], P(('dp', 'seq'))
- grad_attn_gain: float32 [2560], P(('dp', 'seq'))
- grad_ffn_gain: float32 [2560], P(('dp', 'seq'))
The draws below stay inside these ranges and needn't reach their ends.
All inputs are finite; a program needn't handle non-finite values.
Results may differ from the reference program's by a relative error of at most 0.013.
The reference program's roundings to bfloat16 on the way count: a program that leaves them out, or rounds other values in their place, can miss the bound.
Values may be sent and summed in bfloat16 or wider, within the bound.
No kernel may reach another device: no remote copies, remote signals or barrier semaphores. Data moves between devices by JAX's collectives and lax.ppermute only.
A program may use at most 704 MiB of HBM per device.

```python
import math
import jax
import jax.numpy as jnp
from jax import lax

D = 2560
HEADS = 5
HEAD = 256
FF = 3840
WINDOW = 2048
CH = 192
SEQS = 4
LEN = 1536
REACH = 11


def draw_block_input(key, part):
    subkeys = jax.random.split(jax.random.fold_in(key, 101), 3)
    row_scale = jnp.exp(jax.random.uniform(subkeys[0], (SEQS, LEN, 1), minval=0.0, maxval=math.log(10.0)))
    result = jax.random.truncated_normal(subkeys[2], -4.0, 4.0, (SEQS, LEN, D)) * row_scale
    return result.astype(jnp.bfloat16)


def draw_qkv_weight(key, part):
    fold_key = jax.random.fold_in(key, 202)
    draw_shape = (D, HEADS * HEAD + 2 * HEAD)
    matrix = jax.random.truncated_normal(fold_key, -4.0, 4.0, draw_shape) * D ** (-0.5)
    return matrix.astype(jnp.bfloat16)


def with_spikes(values, own_key, source, target, parts, factor):
    owner, partner = [(jnp.arange(values.shape[position]) // (values.shape[position] // parts)).reshape([-1 if axis == position else 1 for axis in range(values.ndim)]) for position in (source, target)]
    chosen = jax.random.permutation(own_key, parts)[partner]
    strong = (owner == chosen) | (owner == (partner + parts // 2) % parts)
    return jnp.where(strong, factor * values, values)


def levels(rng, dims, shards, least, high):
    level = 1.0
    for position, blocks in shards:
        draws = jax.random.uniform(jax.random.fold_in(jax.random.fold_in(rng, 6), position), (blocks,), jnp.float32, least / len(shards), high / len(shards))
        level = level * jnp.repeat(jnp.exp(draws), dims[position] // blocks).reshape((-1,) + (1,) * (len(dims) - 1 - position))
    return level


def centred(own_key, extent, spread, most, cuts=(), kind=jnp.bfloat16):
    entries = spread * jax.random.normal(own_key, extent, jnp.float32)
    if cuts:
        entries = entries * levels(own_key, extent, cuts, -0.22, 0.18)
    return jnp.clip(entries, -most, most).astype(kind)


def gaussian_with(rng, dims, scale, most, cuts, heavy, kind=jnp.bfloat16):
    values = scale * jax.random.normal(rng, dims, jnp.float32)
    if cuts:
        values = values * levels(rng, dims, cuts, -0.22, 0.18)
    return jnp.clip(with_spikes(values, jax.random.fold_in(rng, 3), *heavy), -most, most).astype(kind)


def setup_inputs(seed: int = 0) -> dict:
    key_list = jax.random.split(jax.random.key(seed), 9)
    return {
        "block_input": draw_block_input(jax.random.fold_in(key_list[8], 71), 0),
        "qkv_weight": draw_qkv_weight(jax.random.fold_in(key_list[8], 71), 0),
        "out_weight": centred(key_list[2], (D, HEADS * HEAD), (max(1, (HEADS * HEAD) // (WINDOW // 2))) ** -0.5, 6.0, ((0, 32),)),
        "ffn_weight": centred(key_list[3], (D, 2 * FF), D ** -0.5, 0.125, ((0, 32),)),
        "down_weight": centred(key_list[4], (D, FF), FF ** -0.5, 0.09375, ((0, 32),)),
        "attn_gain": jnp.clip(1.0 + 0.18 * jax.random.normal(key_list[5], (D,), jnp.float32), 0.099609375, 1.8984375).astype(jnp.bfloat16),
        "ffn_gain": jnp.clip(1.0 + 0.18 * jax.random.normal(key_list[6], (D,), jnp.float32), 0.099609375, 1.8984375).astype(jnp.bfloat16),
        "cotangent": gaussian_with(key_list[7], (SEQS, LEN, D), 1.0, 6.0, ((0, 4), (1, 8)), (1, 2, 8, 2.0)),
    }


EPSILON = 1e-06
GELU_C = 0.7978845608028654

def rope_tables(positions):
    half_dim = HEAD // 2
    frequency = 10000.0 ** (-jnp.arange(half_dim, dtype=jnp.float32) / half_dim)
    angles = positions.astype(jnp.float32)[:, None] * frequency[None, :]
    return (jnp.cos(angles), jnp.sin(angles))

def rotate(values, cosine, sine_part):
    half_dim = values.shape[-1] // 2
    first_half = values[..., :half_dim]
    second_half = values[..., half_dim:]
    return jnp.concatenate([first_half * cosine - second_half * sine_part, second_half * cosine + first_half * sine_part], -1)

def unrotate(values, cosine, sine_part):
    half_dim = values.shape[-1] // 2
    first_half = values[..., :half_dim]
    second_half = values[..., half_dim:]
    return jnp.concatenate([first_half * cosine + second_half * sine_part, second_half * cosine - first_half * sine_part], -1)

def gelu_parts(gate_in):
    cubic_term = 0.044715
    inner_arg = GELU_C * (gate_in + cubic_term * gate_in ** 3)
    tangent = jnp.tanh(inner_arg)
    gelu_value = 0.5 * gate_in * (1.0 + tangent)
    gelu_slope = 0.5 * (1.0 + tangent) + 0.5 * gate_in * (1.0 - tangent ** 2) * GELU_C * (1.0 + 3.0 * cubic_term * gate_in ** 2)
    return (gelu_value, gelu_slope)

def visible(query_pos, key_pos):
    later = query_pos[:, None] - key_pos[None, :]
    return (key_pos[None, :] >= 0) & (later >= 0) & (later < WINDOW)

def rounded(values):
    return lax.optimization_barrier(values.astype(jnp.bfloat16)).astype(jnp.float32)

def attend(queries, keys_win, values_win, visible_mask):
    scores = jnp.einsum('qhd,kd->hqk', queries.astype(jnp.float32), keys_win.astype(jnp.float32))
    scores = jnp.where(visible_mask[None], scores, -jnp.inf)
    row_peak = lax.optimization_barrier(jnp.max(scores, -1, keepdims=True))
    log_total = row_peak + jnp.log(lax.optimization_barrier(jnp.sum(jnp.exp(scores - row_peak), -1, keepdims=True)))
    attn_probs = jnp.exp(scores - log_total)
    attn_mixed = jnp.einsum('hqk,kd->qhd', rounded(attn_probs), values_win.astype(jnp.float32))
    return (attn_mixed.astype(jnp.bfloat16), log_total)

def attend_back(queries, keys_win, values_win, visible_mask, log_total, grad_mixed):
    scores = jnp.einsum('qhd,kd->hqk', queries.astype(jnp.float32), keys_win.astype(jnp.float32))
    scores = jnp.where(visible_mask[None], scores, -jnp.inf)
    attn_probs = jnp.exp(scores - log_total)
    grad_values = jnp.einsum('hqk,qhd->kd', rounded(attn_probs), grad_mixed.astype(jnp.float32))
    grad_probs = jnp.einsum('qhd,kd->hqk', grad_mixed.astype(jnp.float32), values_win.astype(jnp.float32))
    row_delta = lax.optimization_barrier(jnp.sum(attn_probs * grad_probs, -1, keepdims=True))
    grad_scores = rounded(attn_probs * (grad_probs - row_delta))
    grad_queries = jnp.einsum('hqk,kd->qhd', grad_scores, keys_win.astype(jnp.float32))
    grad_keys = jnp.einsum('hqk,qhd->kd', grad_scores, queries.astype(jnp.float32))
    return (grad_queries, grad_keys, grad_values)

def reference(block_input, qkv_weight, out_weight, ffn_weight, down_weight, attn_gain, ffn_gain, cotangent):
    width_q = HEADS * HEAD
    win_rows = (REACH + 1) * CH
    margin = REACH * CH
    blocks_count = LEN // CH
    query_scale = HEAD ** (-0.5)
    gain_one = attn_gain.astype(jnp.float32)
    gain_two = ffn_gain.astype(jnp.float32)
    positions = jnp.arange(LEN, dtype=jnp.int32)
    cosine, sine_part = rope_tables(positions)

    def one_sequence(running, pair):
        tokens, cot_rows = pair
        token_f = tokens.astype(jnp.float32)
        inv_one = lax.rsqrt(lax.optimization_barrier(jnp.mean(token_f * token_f, -1, keepdims=True)) + EPSILON)
        normed_one = (token_f * inv_one * gain_one).astype(jnp.bfloat16)
        qkv_rows = jnp.dot(normed_one, qkv_weight, preferred_element_type=jnp.float32)
        queries = (rotate(qkv_rows[:, :width_q].reshape(LEN, HEADS, HEAD), cosine[:, None, :], sine_part[:, None, :]) * query_scale).astype(jnp.bfloat16)
        keys_all = rotate(qkv_rows[:, width_q:width_q + HEAD], cosine, sine_part).astype(jnp.bfloat16)
        values_all = qkv_rows[:, width_q + HEAD:].astype(jnp.bfloat16)
        keys_pad = jnp.concatenate([jnp.zeros((margin, HEAD), jnp.bfloat16), keys_all], 0)
        values_pad = jnp.concatenate([jnp.zeros((margin, HEAD), jnp.bfloat16), values_all], 0)

        def block_parts(block_id):
            first_row = (block_id * CH).astype(jnp.int32)
            query_blk = lax.dynamic_slice_in_dim(queries, first_row, CH, 0)
            keys_win = lax.dynamic_slice_in_dim(keys_pad, first_row, win_rows, 0)
            values_win = lax.dynamic_slice_in_dim(values_pad, first_row, win_rows, 0)
            query_pos = first_row + jnp.arange(CH, dtype=jnp.int32)
            key_pos = first_row - margin + jnp.arange(win_rows, dtype=jnp.int32)
            return (first_row, query_blk, keys_win, values_win, visible(query_pos, key_pos))

        def forward_block(block_id):
            first_row, query_blk, keys_win, values_win, visible_mask = block_parts(block_id)
            return attend(query_blk, keys_win, values_win, visible_mask)
        mixed_all, log_totals = lax.map(forward_block, jnp.arange(blocks_count, dtype=jnp.int32))
        attn_flat = mixed_all.reshape(LEN, width_q)
        hidden_one = token_f + jnp.dot(attn_flat, out_weight.T, preferred_element_type=jnp.float32)
        inv_two = lax.rsqrt(lax.optimization_barrier(jnp.mean(hidden_one * hidden_one, -1, keepdims=True)) + EPSILON)
        normed_two = (hidden_one * inv_two * gain_two).astype(jnp.bfloat16)
        gate_up = jnp.dot(normed_two, ffn_weight, preferred_element_type=jnp.float32)
        gelu_value, gelu_slope = gelu_parts(gate_up[:, :FF])
        up_part = gate_up[:, FF:]
        hidden = (gelu_value * up_part).astype(jnp.bfloat16)
        output_rows = (hidden_one + jnp.dot(hidden, down_weight.T, preferred_element_type=jnp.float32)).astype(jnp.bfloat16)
        grad_hidden = jnp.dot(cot_rows, down_weight, preferred_element_type=jnp.float32)
        grad_gate_up = jnp.concatenate([grad_hidden * up_part * gelu_slope, grad_hidden * gelu_value], -1).astype(jnp.bfloat16)
        grad_norm_two = jnp.dot(grad_gate_up, ffn_weight.T, preferred_element_type=jnp.float32)
        gain_two_grad = lax.optimization_barrier(jnp.sum(grad_norm_two * hidden_one * inv_two, 0))
        scaled_two = gain_two * grad_norm_two
        grad_h_one = cot_rows.astype(jnp.float32) + inv_two * scaled_two - hidden_one * inv_two ** 3 * lax.optimization_barrier(jnp.mean(scaled_two * hidden_one, -1, keepdims=True))
        grad_h_bf = grad_h_one.astype(jnp.bfloat16)
        grad_attn = jnp.dot(grad_h_bf, out_weight, preferred_element_type=jnp.float32).astype(jnp.bfloat16).reshape(LEN, HEADS, HEAD)

        def backward_block(grad_pad, block_id):
            first_row, query_blk, keys_win, values_win, visible_mask = block_parts(block_id)
            grad_blk = lax.dynamic_slice_in_dim(grad_attn, first_row, CH, 0)
            grad_queries, grad_keys, grad_values = attend_back(query_blk, keys_win, values_win, visible_mask, log_totals[block_id], grad_blk)
            current = lax.dynamic_slice_in_dim(grad_pad, first_row, win_rows, 0)
            grad_pad = lax.dynamic_update_slice_in_dim(grad_pad, current + jnp.concatenate([grad_keys, grad_values], -1), first_row, 0)
            return (grad_pad, grad_queries)
        grad_pad, grad_q_blocks = lax.scan(backward_block, jnp.zeros((margin + LEN, 2 * HEAD), jnp.float32), jnp.arange(blocks_count, dtype=jnp.int32))
        grad_kv = grad_pad[margin:]
        grad_query = unrotate(grad_q_blocks.reshape(LEN, HEADS, HEAD), cosine[:, None, :], sine_part[:, None, :]) * query_scale
        grad_key = unrotate(grad_kv[:, :HEAD], cosine, sine_part)
        grad_qkv_rows = jnp.concatenate([grad_query.reshape(LEN, width_q), grad_key, grad_kv[:, HEAD:]], -1).astype(jnp.bfloat16)
        grad_norm_one = jnp.dot(grad_qkv_rows, qkv_weight.T, preferred_element_type=jnp.float32)
        gain_one_grad = lax.optimization_barrier(jnp.sum(grad_norm_one * token_f * inv_one, 0))
        scaled_one = gain_one * grad_norm_one
        grad_rows = grad_h_one + inv_one * scaled_one - token_f * inv_one ** 3 * lax.optimization_barrier(jnp.mean(scaled_one * token_f, -1, keepdims=True))
        new_running = (running[0] + jnp.dot(normed_one.T, grad_qkv_rows, preferred_element_type=jnp.float32), running[1] + jnp.dot(grad_h_bf.T, attn_flat, preferred_element_type=jnp.float32), running[2] + jnp.dot(normed_two.T, grad_gate_up, preferred_element_type=jnp.float32), running[3] + jnp.dot(cot_rows.T, hidden, preferred_element_type=jnp.float32), running[4] + gain_one_grad, running[5] + gain_two_grad)
        return (new_running, (output_rows, grad_rows))
    initial = (jnp.zeros((D, width_q + 2 * HEAD), jnp.float32), jnp.zeros((D, width_q), jnp.float32), jnp.zeros((D, 2 * FF), jnp.float32), jnp.zeros((D, FF), jnp.float32), jnp.zeros((D,), jnp.float32), jnp.zeros((D,), jnp.float32))
    totals, results = lax.scan(one_sequence, initial, (block_input, cotangent))
    return (results[0], results[1], totals[0], totals[1], totals[2], totals[3], totals[4], totals[5])
```

```python
import jax
import jax.numpy as jnp
from jax import lax
from jax.experimental import pallas as pl
from jax.experimental.pallas import tpu as pltpu
from jax.sharding import Mesh, PartitionSpec as P


HEADS = 5
HEAD = 256
FF = 3840
WINDOW = 2048


EPSILON = 1e-06
GELU_C = 0.7978845608028654
CORES = 2
EVERY = ("da", "db", "z", "core")
SEQ = ("z", "core")
PAIR = ("da", "db")
PLANE = ("da", "db", "core")
LANES = 128
BF = jnp.bfloat16
F32 = jnp.float32


def rope_tables(positions):
    half_dim = HEAD // 2
    frequency = 10000.0 ** (-jnp.arange(half_dim, dtype=jnp.float32) / half_dim)
    angles = positions.astype(jnp.float32)[:, None] * frequency[None, :]
    return (jnp.cos(angles), jnp.sin(angles))


def rotate(values, cosine, sine_part):
    half_dim = values.shape[-1] // 2
    first_half = values[..., :half_dim]
    second_half = values[..., half_dim:]
    return jnp.concatenate(
        [
            first_half * cosine - second_half * sine_part,
            second_half * cosine + first_half * sine_part,
        ],
        -1,
    )


def unrotate(values, cosine, sine_part):
    half_dim = values.shape[-1] // 2
    first_half = values[..., :half_dim]
    second_half = values[..., half_dim:]
    return jnp.concatenate(
        [
            first_half * cosine + second_half * sine_part,
            second_half * cosine - first_half * sine_part,
        ],
        -1,
    )


def gelu_parts(gate_in):
    cubic_term = 0.044715
    inner_arg = GELU_C * (gate_in + cubic_term * gate_in**3)
    tangent = jnp.tanh(inner_arg)
    gelu_value = 0.5 * gate_in * (1.0 + tangent)
    gelu_slope = 0.5 * (1.0 + tangent) + 0.5 * gate_in * (1.0 - tangent**2) * GELU_C * (
        1.0 + 3.0 * cubic_term * gate_in**2
    )
    return (gelu_value, gelu_slope)


def contract_rows(left_rows, right_rows):
    return lax.dot_general(
        left_rows, right_rows, (((0,), (0,)), ((), ())), preferred_element_type=jnp.float32
    )


def contract_cols(left_rows, right_rows):
    return lax.dot_general(
        left_rows, right_rows, (((1,), (1,)), ((), ())), preferred_element_type=jnp.float32
    )


def gather(values, axes, axis=0, tiled=True):
    return lax.all_gather(values, axes, axis=axis, tiled=tiled)


def scatter(values, axes, axis=0):
    return lax.psum_scatter(values, axes, scatter_dimension=axis, tiled=True)


def exchange(values, axes):
    return lax.all_to_all(values, axes, split_axis=0, concat_axis=0, tiled=True)


def shift(values, axis, step):
    count = lax.axis_size(axis)
    return lax.ppermute(values, axis, [(i, (i + step) % count) for i in range(count)])


def slide(values, axis, step):
    count = lax.axis_size(axis)
    pairs = [(i, i + step) for i in range(count) if 0 <= i + step < count]
    return lax.ppermute(values, axis, pairs)


def pick(values, index, axis):
    return lax.dynamic_index_in_dim(values, index, axis, keepdims=False)


def line_gather(values, axis):
    count = lax.axis_size(axis)
    here = lax.axis_index(axis)
    right, left = values, values
    rights, lefts = [], []
    for _ in range(1, count):
        right = slide(right, axis, 1)
        left = slide(left, axis, -1)
        rights.append(right)
        lefts.append(left)
    pieces = [values]
    for k in range(1, count):
        pieces.append(jnp.where(here >= k, rights[k - 1], lefts[count - k - 1]))
    return pieces


def place(pieces, here, dim):
    count = len(pieces)
    shape = list(pieces[0].shape)
    shape.insert(dim, count)
    buffer = jnp.zeros(shape, pieces[0].dtype)
    for k, piece in enumerate(pieces):
        at = [0] * len(shape)
        at[dim] = (here - k) % count
        buffer = lax.dynamic_update_slice(buffer, jnp.expand_dims(piece, dim), at)
    return buffer


def reduce_axis(values, axis, dim):
    count = lax.axis_size(axis)
    here = lax.axis_index(axis)
    total = pick(values, here, dim).astype(F32)
    for k in range(1, count):
        piece = pick(values, (here + k) % count, dim).astype(BF)
        piece = shift(piece, axis, k)
        total = total + piece.astype(F32)
    return total


def reduce_plane(values, cut):
    half = values.shape[cut] // 2
    first, second = (lax.slice_in_dim(values, i * half, (i + 1) * half, axis=cut) for i in (0, 1))
    first = reduce_axis(reduce_axis(first, "db", 1), "da", 0)
    second = reduce_axis(reduce_axis(second, "da", 0), "db", 0)
    return jnp.concatenate([first, second], cut - 2)


def reduce_rows(term, owned_rows, cut):
    count_a, count_b, count_z = (lax.axis_size(axis) for axis in ("da", "db", "z"))
    columns = term.shape[1]
    blocks = term.reshape(count_a, count_b, CORES, count_z * owned_rows, columns)
    paired = reduce_axis(blocks, "core", 2)
    plane = reduce_plane(paired.astype(BF), cut)
    return reduce_axis(plane.reshape(count_z, owned_rows, columns), "z", 0)


def reduce_tokens(own, other, rows_here, cut):
    count_a, count_b = (lax.axis_size(axis) for axis in PAIR)
    width = own.shape[1]
    other = shift(other, "core", 1)
    paired = (own.astype(F32) + other.astype(F32)).astype(BF)
    return reduce_plane(paired.reshape(count_a, count_b, rows_here, width), cut)


def plane_gather(values):
    count_a, count_b = (lax.axis_size(axis) for axis in PAIR)
    count = count_a * count_b
    here_a, here_b, core = (lax.axis_index(axis) for axis in PLANE)
    rows, width = values.shape
    buffer = jnp.zeros((count_a, count_b, CORES, rows, width), values.dtype)
    for ka in range(count_a):
        for kb in range(count_b):
            piece = values
            if ka or kb:
                pairs = [
                    (
                        i,
                        (i // count_b + ka) % count_a * count_b + (i % count_b + kb) % count_b,
                    )
                    for i in range(count)
                ]
                piece = lax.ppermute(values, PAIR, pairs)
            other = shift(piece, "core", 1)
            at_a, at_b = (here_a - ka) % count_a, (here_b - kb) % count_b
            for part, at in ((piece, core), (other, 1 - core)):
                buffer = lax.dynamic_update_slice(
                    buffer, part[None, None, None], (at_a, at_b, at, 0, 0)
                )
    return buffer.reshape(count * CORES * rows, width)


def hidden_cuts(total, group, part):
    return [
        (min(j * part, total), max(0, min(part, total - j * part))) for j in range(group)
    ]


def pack_shares(ffn_weight, down_weight, group, part):
    rows, total = down_weight.shape
    cuts = hidden_cuts(total, group, part)

    def kernel(ffn_ref, down_ref, out_ref):
        for j, (first, count) in enumerate(cuts):
            if count < part:
                out_ref[j] = jnp.zeros((rows, 3 * part), BF)
            if count:
                out_ref[j, :, pl.ds(0, count)] = ffn_ref[:, pl.ds(first, count)]
                out_ref[j, :, pl.ds(part, count)] = ffn_ref[:, pl.ds(total + first, count)]
                out_ref[j, :, pl.ds(2 * part, count)] = down_ref[:, pl.ds(first, count)]

    return pl.pallas_call(
        kernel,
        out_shape=jax.ShapeDtypeStruct((group, rows, 3 * part), BF),
        name="pack_shares",
    )(ffn_weight, down_weight)


def unpack_gate_up(summed, ffn_weight, ffn_gain, group, part):
    rows, double = ffn_weight.shape
    total = double // 2
    cuts = hidden_cuts(total, group, part)

    def kernel(sum_ref, weight_ref, gain_ref, out_ref, gain_out_ref):
        gain_sum = jnp.zeros((rows, 1), F32)
        for j, (first, count) in enumerate(cuts):
            if count:
                for source, target in ((0, first), (part, total + first)):
                    piece = sum_ref[j, :, pl.ds(source, count)].astype(F32)
                    out_ref[:, pl.ds(target, count)] = piece
                    weight = weight_ref[:, pl.ds(target, count)].astype(F32)
                    gain_sum = gain_sum + jnp.sum(piece * weight, 1, keepdims=True)
        gain_out_ref[...] = gain_sum / gain_ref[...].astype(F32)

    return pl.pallas_call(
        kernel,
        out_shape=(
            jax.ShapeDtypeStruct((rows, double), F32),
            jax.ShapeDtypeStruct((rows, 1), F32),
        ),
        name="unpack_gate_up",
    )(summed, ffn_weight, ffn_gain[:, None])


def unpack_down(summed, total, group, part):
    rows = summed.shape[1]
    cuts = hidden_cuts(total, group, part)

    def kernel(sum_ref, out_ref):
        for j, (first, count) in enumerate(cuts):
            if count:
                out_ref[:, pl.ds(first, count)] = sum_ref[j, :, pl.ds(0, count)].astype(F32)

    return pl.pallas_call(
        kernel, out_shape=jax.ShapeDtypeStruct((rows, total), F32), name="unpack_down"
    )(summed)


def reorder(values, dp_count, first_count, second_count, addend=None, kind=None):
    rows, width = values.shape
    owned = width // (dp_count * first_count * second_count)
    kind = kind or values.dtype

    def kernel(*refs):
        out_ref = refs[-1]
        for d in range(dp_count):
            for i in range(first_count):
                for j in range(second_count):
                    source = pl.ds(((d * first_count + i) * second_count + j) * owned, owned)
                    target = pl.ds(((d * second_count + j) * first_count + i) * owned, owned)
                    piece = refs[0][:, source]
                    if addend is not None:
                        piece = piece + refs[1][:, source]
                    out_ref[:, target] = piece.astype(kind)

    operands = (values,) if addend is None else (values, addend)
    return pl.pallas_call(
        kernel, out_shape=jax.ShapeDtypeStruct((rows, width), kind), name="reorder"
    )(*operands)


def attend(rows_in, kv_pieces, cosine, sine_part, query_pos, key_pos):
    rows = rows_in.shape[0]
    query_scale = HEAD ** (-0.5)
    count = len(kv_pieces)
    length = count * rows

    def kernel(*refs):
        kv_refs = refs[:count]
        q_ref, cos_ref, sin_ref, qp_ref, kp_ref, out_ref, lse_ref, qr_ref, kv_all = refs[count:]
        for i, ref in enumerate(kv_refs):
            kv_all[pl.ds(i * rows, rows), :] = ref[...]
        later = qp_ref[...] - kp_ref[...]
        seen = (later >= 0) & (later < WINDOW)
        lanes = lax.broadcasted_iota(jnp.int32, (rows, LANES), 1)
        totals = jnp.zeros((rows, LANES), F32)
        for h in range(HEADS):
            at = pl.ds(h * HEAD, HEAD)
            rotated = rotate(q_ref[:, at], cos_ref[...], sin_ref[...])
            query = (rotated * query_scale).astype(BF)
            qr_ref[:, at] = query
            scores = jnp.where(seen, contract_cols(query, kv_all[:, :HEAD]), -jnp.inf)
            peak = jnp.max(scores, -1, keepdims=True)
            weights = jnp.exp(scores - peak)
            total = jnp.sum(weights, -1, keepdims=True)
            probs = (weights * (1.0 / total)).astype(BF)
            mixed = jnp.dot(probs, kv_all[:, HEAD:], preferred_element_type=F32)
            out_ref[:, at] = mixed.astype(BF)
            totals = jnp.where(lanes == h, peak + jnp.log(total), totals)
        lse_ref[...] = totals

    return pl.pallas_call(
        kernel,
        out_shape=(
            jax.ShapeDtypeStruct((rows, HEADS * HEAD), BF),
            jax.ShapeDtypeStruct((rows, LANES), F32),
            jax.ShapeDtypeStruct((rows, HEADS * HEAD), BF),
        ),
        scratch_shapes=[pltpu.VMEM((length, 2 * HEAD), BF)],
        cost_estimate=pl.CostEstimate(
            flops=4 * rows * length * HEADS * HEAD,
            transcendentals=rows * length * HEADS,
            bytes_accessed=4 * length * HEAD + 10 * rows * HEADS * HEAD,
        ),
        name="attend",
    )(*kv_pieces, rows_in, cosine, sine_part, query_pos, key_pos)


def attend_back(queries, kv_pieces, cosine, sine_part, query_pos, key_pos, totals, grad_mixed):
    rows = queries.shape[0]
    count = len(kv_pieces)
    length = count * rows
    half = length // 2
    query_scale = HEAD ** (-0.5)

    def kernel(*refs):
        kv_refs = refs[:count]
        q_ref, cos_ref, sin_ref, qp_ref, kp_ref, lse_ref, do_ref = refs[count : count + 7]
        dq_ref, own_ref, other_ref, kv_all, ds_all, probs_all, q_all, do_all = refs[count + 7 :]
        for i, ref in enumerate(kv_refs):
            kv_all[pl.ds(i * rows, rows), :] = ref[...]
        later = qp_ref[...] - kp_ref[...]
        seen = (later >= 0) & (later < WINDOW)
        for h in range(HEADS):
            at = pl.ds(h * HEAD, HEAD)
            below = pl.ds(h * rows, rows)
            query = q_ref[:, at]
            grad_out = do_ref[:, at]
            scores = jnp.where(seen, contract_cols(query, kv_all[:, :HEAD]), -jnp.inf)
            probs = jnp.exp(scores - lse_ref[:, h : h + 1])
            grad_probs = contract_cols(grad_out, kv_all[:, HEAD:])
            delta = jnp.sum(probs * grad_probs, -1, keepdims=True)
            grad_scores = (probs * (grad_probs - delta)).astype(BF)
            ds_all[below, :] = grad_scores
            probs_all[below, :] = probs.astype(BF)
            q_all[below, :] = query
            do_all[below, :] = grad_out
            grad_query = jnp.dot(grad_scores, kv_all[:, :HEAD], preferred_element_type=F32)
            grad_query = unrotate(grad_query, cos_ref[...], sin_ref[...]) * query_scale
            dq_ref[:, at] = grad_query.astype(BF)
        for ref, first, kind in ((own_ref, 0, F32), (other_ref, half, BF)):
            part = pl.ds(first, half)
            ref[:, :HEAD] = contract_rows(ds_all[:, part], q_all[...]).astype(kind)
            ref[:, HEAD:] = contract_rows(probs_all[:, part], do_all[...]).astype(kind)

    stacked = HEADS * rows
    return pl.pallas_call(
        kernel,
        out_shape=(
            jax.ShapeDtypeStruct((rows, HEADS * HEAD), BF),
            jax.ShapeDtypeStruct((half, 2 * HEAD), F32),
            jax.ShapeDtypeStruct((half, 2 * HEAD), BF),
        ),
        scratch_shapes=[
            pltpu.VMEM((length, 2 * HEAD), BF),
            pltpu.VMEM((stacked, length), BF),
            pltpu.VMEM((stacked, length), BF),
            pltpu.VMEM((stacked, HEAD), BF),
            pltpu.VMEM((stacked, HEAD), BF),
        ],
        cost_estimate=pl.CostEstimate(
            flops=10 * rows * length * HEADS * HEAD,
            transcendentals=rows * length * HEADS,
            bytes_accessed=7 * length * HEAD + 10 * rows * HEADS * HEAD,
        ),
        name="attend_back",
    )(*kv_pieces, queries, cosine, sine_part, query_pos, key_pos, totals, grad_mixed)


def plane_specs(dp_count, rows_here):
    together = 2
    steps = dp_count // together

    def tokens(columns):
        return pl.BlockSpec(
            (together, 1, rows_here, columns),
            lambda i, core: (i % steps, jnp.where(i < steps, 1 - core[0], core[0]), 0, 0),
        )

    def halves(columns):
        rows = together * rows_here
        return (
            pl.BlockSpec((rows, columns), lambda i, core: (jnp.minimum(i, steps - 1), 0)),
            pl.BlockSpec((rows, columns), lambda i, core: (jnp.maximum(i - steps, 0), 0)),
        )

    return steps, together * rows_here, tokens, halves


def feed_forward(core, tokens_in, weight, grad_hidden):
    dp_count, _, rows_here, width = tokens_in.shape
    part = grad_hidden.shape[3]
    steps, rows, tokens, halves = plane_specs(dp_count, rows_here)

    def kernel(core_ref, in_ref, weight_ref, grad_ref, hid_ref, dgu_ref, other_ref, own_ref):
        step = pl.program_id(0)
        both = jnp.dot(in_ref[...].reshape(rows, width), weight_ref[...], preferred_element_type=F32)
        gelu_value, gelu_slope = gelu_parts(both[:, :part])
        up_part = both[:, part:]
        grad = grad_ref[...].reshape(rows, part)
        hid_ref[...] = (gelu_value * up_part).astype(BF).reshape(hid_ref.shape)
        dgu = jnp.concatenate([grad * up_part * gelu_slope, grad * gelu_value], 1).astype(BF)
        dgu_ref[...] = dgu.reshape(dgu_ref.shape)
        term = contract_cols(dgu, weight_ref[...]).astype(BF)

        @pl.when(step < steps)
        def _():
            other_ref[...] = term

        @pl.when(step >= steps)
        def _():
            own_ref[...] = term

    count = dp_count * CORES * rows_here
    half = jax.ShapeDtypeStruct((count // 2, width), BF)
    return pl.pallas_call(
        kernel,
        grid_spec=pltpu.PrefetchScalarGridSpec(
            num_scalar_prefetch=1,
            grid=(2 * steps,),
            in_specs=[
                tokens(width),
                pl.BlockSpec((width, 2 * part), lambda i, core: (0, 0)),
                tokens(part),
            ],
            out_specs=(tokens(part), tokens(2 * part), *halves(width)),
        ),
        out_shape=(
            jax.ShapeDtypeStruct((dp_count, CORES, rows_here, part), BF),
            jax.ShapeDtypeStruct((dp_count, CORES, rows_here, 2 * part), BF),
            half,
            half,
        ),
        cost_estimate=pl.CostEstimate(
            flops=8 * count * width * part,
            transcendentals=count * part,
            bytes_accessed=4 * count * width + 4 * width * part + 10 * count * part,
        ),
        name="feed_forward",
    )(core, tokens_in, weight, grad_hidden)


def down_product(core, hidden, weight):
    dp_count, _, rows_here, part = hidden.shape
    width = weight.shape[0]
    steps, rows, tokens, halves = plane_specs(dp_count, rows_here)

    def kernel(core_ref, in_ref, weight_ref, other_ref, own_ref):
        step = pl.program_id(0)
        term = contract_cols(in_ref[...].reshape(rows, part), weight_ref[...]).astype(BF)

        @pl.when(step < steps)
        def _():
            other_ref[...] = term

        @pl.when(step >= steps)
        def _():
            own_ref[...] = term

    count = dp_count * CORES * rows_here
    half = jax.ShapeDtypeStruct((count // 2, width), BF)
    return pl.pallas_call(
        kernel,
        grid_spec=pltpu.PrefetchScalarGridSpec(
            num_scalar_prefetch=1,
            grid=(2 * steps,),
            in_specs=[tokens(part), pl.BlockSpec((width, part), lambda i, core: (0, 0))],
            out_specs=halves(width),
        ),
        out_shape=(half, half),
        cost_estimate=pl.CostEstimate(
            flops=2 * count * width * part,
            transcendentals=0,
            bytes_accessed=2 * count * (width + part) + 2 * width * part,
        ),
        name="down_product",
    )(core, hidden, weight)


def weight_term(left, right, dp_count, z_count):
    tokens, width = left.shape
    columns = right.shape[1]
    per_dp = width // dp_count
    owned = per_dp // (z_count * CORES)
    together = 1
    while (together * per_dp) % LANES:
        together *= 2
    block = together * per_dp

    def kernel(left_ref, right_ref, out_ref):
        term = contract_rows(left_ref[...], right_ref[...]).astype(BF)
        for d in range(together):
            for c in range(CORES):
                for z in range(z_count):
                    first = d * per_dp + (c * z_count + z) * owned
                    out_ref[z, d, c] = term[first : first + owned]

    return pl.pallas_call(
        kernel,
        grid=(width // block,),
        in_specs=[
            pl.BlockSpec((tokens, block), lambda i: (0, i)),
            pl.BlockSpec((tokens, columns), lambda i: (0, 0)),
        ],
        out_specs=pl.BlockSpec(
            (z_count, together, CORES, owned, columns), lambda i: (0, i, 0, 0, 0)
        ),
        out_shape=jax.ShapeDtypeStruct((z_count, dp_count, CORES, owned, columns), BF),
        cost_estimate=pl.CostEstimate(
            flops=2 * tokens * width * columns,
            transcendentals=0,
            bytes_accessed=2 * (tokens * width + tokens * columns + width * columns),
        ),
        name="weight_term",
    )(left, right)


def body(
    block_input, qkv_weight, out_weight, ffn_weight, down_weight, attn_gain, ffn_gain, cotangent
):
    tokens = block_input[0]
    cot_rows = cotangent[0]
    rows_here, width = tokens.shape
    owned_rows = qkv_weight.shape[0]
    dp_count = lax.axis_size("da") * lax.axis_size("db")
    z_count = lax.axis_size("z")
    z_index = lax.axis_index("z")
    core = lax.axis_index("core")
    group = dp_count * CORES
    width_q = HEADS * HEAD
    width_qkv = width_q + 2 * HEAD
    part = -(-FF // (LANES * group)) * LANES

    tokens = reorder(tokens, dp_count, z_count, CORES)
    cot_rows = reorder(cot_rows, dp_count, z_count, CORES)

    gain_columns = jnp.stack([attn_gain, ffn_gain], 1)
    gain_columns = jnp.pad(gain_columns, ((0, 0), (0, LANES - 2)))
    qkv_line = gather(jnp.concatenate([qkv_weight, gain_columns], 1), "z")
    packed = pack_shares(ffn_weight, down_weight, group, part)
    mine = exchange(packed, PLANE)
    qkv_line, mine, out_weight = lax.optimization_barrier((qkv_line, mine, out_weight))
    share = group // 2
    gate_up_w = jnp.zeros((group, z_count, owned_rows, 2 * part), BF)
    down_w = jnp.zeros((group, z_count, owned_rows, part), BF)
    for i in range(2):
        pieces = line_gather(mine[i * share : (i + 1) * share, None], "z")
        for k, piece in enumerate(pieces):
            at = (i * share, (z_index - k) % z_count, 0, 0)
            gate_up_w = lax.dynamic_update_slice(gate_up_w, piece[..., : 2 * part], at)
            down_w = lax.dynamic_update_slice(down_w, piece[..., 2 * part :], at)
    gate_up_w = gate_up_w.reshape(width, 2 * part)
    down_w = down_w.reshape(width, part)
    qkv_gain = gather(qkv_line, PLANE)
    qkv_full = qkv_gain[:, :width_qkv]
    gain_one = qkv_gain[:, width_qkv].astype(F32)
    gain_two = qkv_gain[:, width_qkv + 1].astype(F32)
    out_pieces = [out_weight] + [shift(out_weight, "z", k) for k in range(1, z_count)]
    out_line = place(out_pieces, z_index, 0).reshape(z_count * owned_rows, width_q)
    out_full = plane_gather(out_line)
    cot_plane = plane_gather(cot_rows)

    positions = (z_index * CORES + core) * rows_here + jnp.arange(rows_here, dtype=jnp.int32)
    cosine, sine_part = rope_tables(positions)
    token_f = tokens.astype(jnp.float32)
    inv_one = lax.rsqrt(jnp.mean(token_f * token_f, -1, keepdims=True) + EPSILON)
    normed_one = (token_f * inv_one * gain_one).astype(jnp.bfloat16)
    qkv_rows = jnp.dot(normed_one, qkv_full, preferred_element_type=jnp.float32)
    keys_own = rotate(qkv_rows[:, width_q : width_q + HEAD], cosine, sine_part).astype(jnp.bfloat16)
    kv_rows = jnp.concatenate([keys_own, qkv_rows[:, width_q + HEAD :].astype(jnp.bfloat16)], -1)
    kv_pieces = [kv_rows] + [shift(kv_rows, "z", k) for k in range(1, z_count)]
    kv_pieces = kv_pieces + [shift(piece, "core", 1) for piece in kv_pieces]
    block_z = (z_index - jnp.arange(z_count, dtype=jnp.int32)) % z_count
    block_at = jnp.concatenate([block_z * CORES + core, block_z * CORES + (1 - core)])
    key_pos = (
        block_at[:, None] * rows_here + jnp.arange(rows_here, dtype=jnp.int32)[None, :]
    ).reshape(1, -1)
    query_pos = positions[:, None]
    attn_flat, log_total, queries = attend(
        qkv_rows, kv_pieces, cosine, sine_part, query_pos, key_pos
    )
    hidden_one = token_f + contract_cols(attn_flat, out_full)
    inv_two = lax.rsqrt(jnp.mean(hidden_one * hidden_one, -1, keepdims=True) + EPSILON)
    normed_two = (hidden_one * inv_two * gain_two).astype(jnp.bfloat16)

    normed_plane = gather(normed_two, PLANE)
    grad_hidden = jnp.dot(cot_plane, down_w, preferred_element_type=jnp.float32)
    core_at = jnp.full((1,), core, jnp.int32)
    in_blocks = (dp_count, CORES, rows_here, -1)
    hidden, grad_gate_up, dn2_other, dn2_own = feed_forward(
        core_at, normed_plane.reshape(in_blocks), gate_up_w, grad_hidden.reshape(in_blocks)
    )
    grad_norm_two = reduce_tokens(dn2_own, dn2_other, rows_here, 2)
    down_other, down_own = down_product(core_at, hidden, down_w)
    down_rows = reduce_tokens(down_own, down_other, rows_here, 3)
    output_rows = reorder(hidden_one, dp_count, CORES, z_count, down_rows, BF)

    def sum_ffn(left, right):
        right = right.reshape(left.shape[0], -1)
        term = weight_term(left, right, dp_count, z_count).reshape(width, right.shape[1])
        mine = scatter(term, "z").reshape(group, owned_rows, right.shape[1])
        return exchange(mine, PLANE)

    gate_up_sum = sum_ffn(normed_plane, grad_gate_up)
    down_sum = sum_ffn(cot_plane, hidden)
    grad_ffn, gain_two_grad = unpack_gate_up(gate_up_sum, ffn_weight, ffn_gain, group, part)
    gain_two_grad = gain_two_grad[:, 0]
    grad_down = unpack_down(down_sum, FF, group, part)

    scaled_two = gain_two * grad_norm_two
    grad_h_one = (
        cot_rows.astype(jnp.float32)
        + inv_two * scaled_two
        - hidden_one * inv_two**3 * jnp.mean(scaled_two * hidden_one, -1, keepdims=True)
    )
    grad_h_bf = grad_h_one.astype(jnp.bfloat16)
    grad_attn = jnp.dot(grad_h_bf, out_full, preferred_element_type=F32).astype(BF)
    grad_query, kv_own, kv_other = attend_back(
        queries, kv_pieces, cosine, sine_part, query_pos, key_pos, log_total, grad_attn
    )
    kv_other = shift(kv_other, "core", 1)
    paired = (kv_own + kv_other.astype(F32)).reshape(z_count, rows_here, 2 * HEAD)
    own_grad = paired[0]
    for k in range(1, z_count):
        piece = paired[k].astype(BF)
        piece = shift(piece, "z", -k)
        own_grad = own_grad + piece.astype(F32)
    grad_key = unrotate(own_grad[:, :HEAD], cosine, sine_part)
    grad_kv = jnp.concatenate([grad_key, own_grad[:, HEAD:]], -1).astype(BF)

    gout_term = contract_rows(grad_h_bf, attn_flat).astype(BF)
    gq_term = contract_rows(normed_one, grad_query).astype(BF)
    gkv_term = contract_rows(normed_one, grad_kv).astype(BF)
    late_kv = grad_kv + 0.0 * gkv_term[0, 0]
    grad_norm_one = contract_cols(jnp.concatenate([grad_query, late_kv], -1), qkv_full)
    scaled_one = gain_one * grad_norm_one
    grad_rows = (
        grad_h_one
        + inv_one * scaled_one
        - token_f * inv_one**3 * jnp.mean(scaled_one * token_f, -1, keepdims=True)
    )
    grad_rows = reorder(grad_rows, dp_count, CORES, z_count)

    grad_out = reduce_rows(gout_term, owned_rows, 3)
    grad_qkv = jnp.concatenate(
        [reduce_rows(gq_term, owned_rows, 2), reduce_rows(gkv_term, owned_rows, 2)],
        1,
    )
    gain_one_grad = jnp.sum(grad_qkv * qkv_weight.astype(F32), 1) / attn_gain.astype(F32)
    return (
        output_rows[None],
        grad_rows[None],
        grad_qkv,
        grad_out,
        grad_ffn,
        grad_down,
        gain_one_grad,
        gain_two_grad,
    )


def solution(mesh):
    dp_count = mesh.shape["dp"]
    seq_count = mesh.shape["seq"]
    split = Mesh(mesh.devices.reshape(dp_count // 2, 2, seq_count // CORES, CORES), EVERY)
    by_token = P(PAIR, SEQ, None)
    by_row = P(EVERY, None)
    by_gain = P(EVERY)


    return jax.shard_map(
        body,
        mesh=split,
        in_specs=(by_token, by_row, by_row, by_row, by_row, by_gain, by_gain, by_token),
        out_specs=(by_token, by_token, by_row, by_row, by_row, by_row, by_gain, by_gain),
        check_vma=False,
    )
```

```python
import jax
import jax.numpy as jnp
from jax import lax
from jax.experimental import pallas as pl
from jax.experimental.pallas import tpu as pltpu
from jax.sharding import Mesh, PartitionSpec as P


HEADS = 5
HEAD = 256
FF = 3840
WINDOW = 2048


EPSILON = 1e-06
GELU_C = 0.7978845608028654
CORES = 2
EVERY = ("da", "db", "z", "core")
SEQ = ("z", "core")
PAIR = ("da", "db")
PLANE = ("da", "db", "core")
LANES = 128
BF = jnp.bfloat16
F32 = jnp.float32


def rope_tables(positions):
    half_dim = HEAD // 2
    frequency = 10000.0 ** (-jnp.arange(half_dim, dtype=jnp.float32) / half_dim)
    angles = positions.astype(jnp.float32)[:, None] * frequency[None, :]
    return (jnp.cos(angles), jnp.sin(angles))


def rotate(values, cosine, sine_part):
    half_dim = values.shape[-1] // 2
    first_half = values[..., :half_dim]
    second_half = values[..., half_dim:]
    return jnp.concatenate(
        [
            first_half * cosine - second_half * sine_part,
            second_half * cosine + first_half * sine_part,
        ],
        -1,
    )


def unrotate(values, cosine, sine_part):
    half_dim = values.shape[-1] // 2
    first_half = values[..., :half_dim]
    second_half = values[..., half_dim:]
    return jnp.concatenate(
        [
            first_half * cosine + second_half * sine_part,
            second_half * cosine - first_half * sine_part,
        ],
        -1,
    )


def gelu_parts(gate_in):
    cubic_term = 0.044715
    inner_arg = GELU_C * (gate_in + cubic_term * gate_in**3)
    tangent = jnp.tanh(inner_arg)
    gelu_value = 0.5 * gate_in * (1.0 + tangent)
    gelu_slope = 0.5 * (1.0 + tangent) + 0.5 * gate_in * (1.0 - tangent**2) * GELU_C * (
        1.0 + 3.0 * cubic_term * gate_in**2
    )
    return (gelu_value, gelu_slope)


def contract_rows(left_rows, right_rows):
    return lax.dot_general(
        left_rows, right_rows, (((0,), (0,)), ((), ())), preferred_element_type=jnp.float32
    )


def contract_cols(left_rows, right_rows):
    return lax.dot_general(
        left_rows, right_rows, (((1,), (1,)), ((), ())), preferred_element_type=jnp.float32
    )


def gather(values, axes, axis=0, tiled=True):
    return lax.all_gather(values, axes, axis=axis, tiled=tiled)


def scatter(values, axes, axis=0):
    return lax.psum_scatter(values, axes, scatter_dimension=axis, tiled=True)


def exchange(values, axes):
    return lax.all_to_all(values, axes, split_axis=0, concat_axis=0, tiled=True)


def shift(values, axis, step):
    count = lax.axis_size(axis)
    return lax.ppermute(values, axis, [(i, (i + step) % count) for i in range(count)])


def slide(values, axis, step):
    count = lax.axis_size(axis)
    pairs = [(i, i + step) for i in range(count) if 0 <= i + step < count]
    return lax.ppermute(values, axis, pairs)


def pick(values, index, axis):
    return lax.dynamic_index_in_dim(values, index, axis, False, allow_negative_indices=False)


def behind(here, step, count):
    return lax.rem(here + (count - step) % count, count)


def line_gather(values, axis):
    right, left = values, values
    rights, lefts = [], []
    for _ in range(1, lax.axis_size(axis)):
        right = slide(right, axis, 1)
        left = slide(left, axis, -1)
        rights.append(right)
        lefts.append(left)
    return rights, lefts


def gather_blocks(pieces, places, rows, count):
    firsts, pieces = zip(*pieces)
    columns = pieces[0].shape[1]
    block = columns
    while block % (2 * LANES) == 0 and block > 1024:
        block //= 2

    def kernel(places_ref, *refs):
        for k, first in enumerate(firsts):
            refs[-1][places_ref[k], pl.ds(first, pieces[k].shape[0])] = refs[k][...]

    return pl.pallas_call(
        kernel,
        grid_spec=pltpu.PrefetchScalarGridSpec(
            num_scalar_prefetch=1,
            grid=(columns // block,),
            in_specs=[
                pl.BlockSpec((piece.shape[0], block), lambda i, at: (0, i)) for piece in pieces
            ],
            out_specs=pl.BlockSpec((count, rows, block), lambda i, at: (0, 0, i)),
        ),
        out_shape=jax.ShapeDtypeStruct((count, rows, columns), pieces[0].dtype),
        cost_estimate=pl.CostEstimate(
            flops=0, transcendentals=0, bytes_accessed=4 * count * rows * columns
        ),
        name="gather_blocks",
    )(jnp.stack(places).astype(jnp.int32), *pieces)


def place_line(z_index, z_count, mine, rights, lefts):
    group, owned, columns = mine.shape
    together = 2

    def kernel(z_ref, mine_ref, *refs):
        out_ref = refs[-1]
        z = z_ref[0]
        out_ref[:, z] = mine_ref[...]
        for k in range(1, z_count):

            @pl.when(z >= k)
            def _():
                out_ref[:, z - k] = refs[k - 1][...]

            @pl.when(z + k < z_count)
            def _():
                out_ref[:, z + k] = refs[z_count + k - 2][...]

    piece = pl.BlockSpec((together, owned, columns), lambda i, z: (i, 0, 0))
    placed = pl.pallas_call(
        kernel,
        grid_spec=pltpu.PrefetchScalarGridSpec(
            num_scalar_prefetch=1,
            grid=(group // together,),
            in_specs=[piece] * (2 * z_count - 1),
            out_specs=pl.BlockSpec(
                (together, z_count, owned, columns), lambda i, z: (i, 0, 0, 0)
            ),
        ),
        out_shape=jax.ShapeDtypeStruct((group, z_count, owned, columns), BF),
        cost_estimate=pl.CostEstimate(
            flops=0, transcendentals=0, bytes_accessed=6 * z_count * group * owned * columns
        ),
        name="place_line",
    )(jnp.full((1,), z_index, jnp.int32), mine, *rights, *lefts)
    return placed.reshape(group * z_count * owned, columns)


def split_rows(rows, row_bytes):
    best = rows
    for block in range(16, rows, 16):
        if rows % block == 0 and block * row_bytes > 3 << 20:
            return block
    return best


def small_kernel(kernel, at, grid, inputs, outputs):
    moved = sum(array.size * array.dtype.itemsize for array, _, _ in (*inputs, *outputs))
    return pl.pallas_call(
        kernel,
        grid_spec=pltpu.PrefetchScalarGridSpec(
            num_scalar_prefetch=1,
            grid=(grid,),
            in_specs=[pl.BlockSpec(block, index) for _, block, index in inputs],
            out_specs=[pl.BlockSpec(block, index) for _, block, index in outputs],
        ),
        out_shape=[shape for shape, _, _ in outputs],
        cost_estimate=pl.CostEstimate(flops=0, transcendentals=0, bytes_accessed=moved),
    )(at, *(array for array, _, _ in inputs))


def pair_split(owns, other, at, which):
    count_a, count_b, rows, columns = other.shape
    half = rows // 2
    block = split_rows(half, 12 * count_a * count_b * columns)
    steps = half // block

    def kernel(at_ref, *refs):
        a, b = at_ref[0], at_ref[1]
        mine, (other_0, other_1), outs = refs[: 2 * len(owns)], refs[2 * len(owns) :][:2], refs[2 * len(owns) + 2 :]
        first = 0
        for n, own in enumerate(owns):
            at_columns = pl.ds(first, own.shape[-1])
            first += own.shape[-1]
            own_0, own_1 = mine[2 * n : 2 * n + 2]
            for k in range(count_b):
                j = lax.rem(b + k, count_b)
                total = own_0[:, j, 0].astype(F32) + other_0[:, j, :, at_columns].astype(F32)
                outs[k][:, :, at_columns] = total.astype(BF)
            for k in range(count_a):
                i = lax.rem(a + k, count_a)
                total = own_1[i, :, 0].astype(F32) + other_1[i, :, :, at_columns].astype(F32)
                outs[count_b + k][:, :, at_columns] = total.astype(BF)

    inputs = [
        (own, (count_a, count_b, 1, block, own.shape[-1]), index)
        for own in owns
        for index in (
            lambda i, at: (0, 0, at[2] if which else 0, i, 0),
            lambda i, at: (0, 0, at[2] if which else 0, i + steps, 0),
        )
    ]
    inputs += [
        (other, (count_a, count_b, block, columns), index)
        for index in (lambda i, at: (0, 0, i, 0), lambda i, at: (0, 0, i + steps, 0))
    ]
    outputs = [
        (
            jax.ShapeDtypeStruct((count, half, columns), BF),
            (count, block, columns),
            lambda i, at: (0, i, 0),
        )
        for count in (count_a,) * count_b + (count_b,) * count_a
    ]
    outs = small_kernel(kernel, at, steps, inputs, outputs)
    return outs[:count_b], outs[count_b:]


def sum_split(kept, arrived, at, axes):
    inputs, outputs = [], []
    for keep, pieces in zip(kept, arrived):
        count, half, columns = keep.shape
        block = split_rows(half, 12 * count * columns)
        for array in (keep, *pieces):
            inputs.append((array, (count, block, columns), lambda i, at: (0, i, 0)))
        for k in range(count):
            shape = jax.ShapeDtypeStruct((half, columns), BF if k else F32)
            outputs.append((shape, (block, columns), lambda i, at: (i, 0)))
    counts = [keep.shape[0] for keep in kept]

    def kernel(at_ref, *refs):
        ins, outs = list(refs[: len(inputs)]), list(refs[len(inputs) :])
        for count, pieces, axis in zip(counts, arrived, axes):
            mine = [ins.pop(0) for _ in range(1 + len(pieces))]
            for k in range(count):
                i = lax.rem(at_ref[axis] + k, count)
                total = mine[0][i].astype(F32)
                for ref in mine[1:]:
                    total = total + ref[i].astype(F32)
                out = outs.pop(0)
                out[...] = total.astype(out.dtype)

    outs = small_kernel(kernel, at, half // block, inputs, outputs)
    return (outs[0], outs[1 : counts[0]]), (outs[counts[0]], outs[counts[0] + 1 :])


def reduce_plane(owns, other, at, which):
    other = shift(other, "core", 1)
    first, second = pair_split(owns, other, at, which)
    arrived = (
        [shift(piece, "db", k + 1) for k, piece in enumerate(first[1:])],
        [shift(piece, "da", k + 1) for k, piece in enumerate(second[1:])],
    )
    (kept_0, sends_0), (kept_1, sends_1) = sum_split((first[0], second[0]), arrived, at, (0, 1))
    arrived_0 = [shift(piece, "da", k + 1) for k, piece in enumerate(sends_0)]
    arrived_1 = [shift(piece, "db", k + 1) for k, piece in enumerate(sends_1)]
    return (kept_0, arrived_0), (kept_1, arrived_1)


def sum_axis(values, axis, dim):
    kept, arrived = send_axis(values, axis, dim)
    for piece in arrived:
        kept = kept + piece.astype(F32)
    return kept


def send_axis(values, axis, dim):
    count = lax.axis_size(axis)
    here = lax.axis_index(axis)
    kept = pick(values, here, dim).astype(F32)
    pieces = [pick(values, behind(here, -k, count), dim).astype(BF) for k in range(1, count)]
    return kept, [shift(piece, axis, k + 1) for k, piece in enumerate(pieces)]


def reduce_plane_fused(own, other):
    other = shift(other, "core", 1)
    paired = (own.astype(F32) + other.astype(F32)).astype(BF)
    half = own.shape[2] // 2
    first = sum_axis(paired[:, :, :half], "db", 1)
    second = sum_axis(paired[:, :, half:], "da", 0)
    return send_axis(first, "da", 0), send_axis(second, "db", 0)


def add_up(refs):
    total = refs[0][...].astype(F32)
    for ref in refs[1:]:
        total = total + ref[...].astype(F32)
    return total


def reduce_tokens(own, other, at):
    count_a, count_b = (lax.axis_size(axis) for axis in PAIR)
    own, other = (x.reshape(count_a, count_b, -1, x.shape[1]) for x in (own, other))
    if at is None:
        return reduce_plane_fused(own, other)
    return reduce_plane((own[:, :, None],), other, at, 0)


def reduce_term(left, right, at):
    count_a, count_b = (lax.axis_size(axis) for axis in PAIR)
    term = contract_rows(left, right).astype(BF)
    term = term.reshape(count_a, count_b, CORES, -1, right.shape[1])
    core = lax.axis_index("core")
    other = pick(term, 1 - core, 2)
    if at is None:
        return reduce_plane_fused(pick(term, core, 2), other)
    return reduce_plane((term,), other, at, 2)


def reduce_line(terms, at, owned):
    count_z = lax.axis_size("z")
    middle = count_z // 2
    widths = [halves[0][0].shape[-1] for halves in terms]
    columns = sum(widths)
    arrays = [
        array.reshape(middle, owned, -1)
        for halves in terms
        for kept, arrived in halves
        for array in (kept, *arrived)
    ]
    splits = [1 + len(arrived) for halves in terms for _, arrived in halves]

    def kernel(at_ref, *refs):
        ins, outs, all_rows = list(refs[: len(arrays)]), refs[len(arrays) : -1], refs[-1]
        first = 0
        for n, size in enumerate(splits):
            width = widths[n // 2]
            start = middle * (n % 2)
            all_rows[start : start + middle, :, first : first + width] = add_up(ins[:size])
            ins = ins[size:]
            first += width * (n % 2)
        for k in range(count_z):
            outs[k][...] = all_rows[lax.rem(at_ref[3] + k, count_z)].astype(outs[k].dtype)

    kept, *sends = pl.pallas_call(
        kernel,
        grid_spec=pltpu.PrefetchScalarGridSpec(
            num_scalar_prefetch=1,
            grid=(1,),
            in_specs=[pl.BlockSpec(array.shape, lambda i, at: (0, 0, 0)) for array in arrays],
            out_specs=[pl.BlockSpec((owned, columns), lambda i, at: (0, 0))] * count_z,
            scratch_shapes=[pltpu.VMEM((count_z, owned, columns), F32)],
        ),
        out_shape=[
            jax.ShapeDtypeStruct((owned, columns), BF if k else F32) for k in range(count_z)
        ],
        name="row_split",
    )(at, *arrays)
    arrived = [shift(piece, "z", k + 1) for k, piece in enumerate(sends)]
    return [kept, *arrived]


def attention_weight_grads(out_terms, qkv_terms, qkv_weight, attn_gain):
    count = len(out_terms)

    def kernel(*refs):
        weight_ref, gain_ref, out_ref, qkv_ref, gain_out_ref = refs[2 * count :]
        out_ref[...] = add_up(refs[:count])
        grad = add_up(refs[count : 2 * count])
        qkv_ref[...] = grad
        gain_sum = jnp.sum(grad * weight_ref[...].astype(F32), 1, keepdims=True)
        gain_out_ref[...] = gain_sum / gain_ref[...].astype(F32)

    rows = qkv_weight.shape[0]
    return pl.pallas_call(
        kernel,
        out_shape=(
            jax.ShapeDtypeStruct(out_terms[0].shape, F32),
            jax.ShapeDtypeStruct(qkv_weight.shape, F32),
            jax.ShapeDtypeStruct((rows, 1), F32),
        ),
        name="attention_weight_grads",
    )(*out_terms, *qkv_terms, qkv_weight, attn_gain[:, None])


def hidden_grads(halves, cot_rows, hidden, inverse, gain):
    rows, width = cot_rows.shape
    half = rows // 2
    block = split_rows(half, 20 * width)
    steps = half // block
    terms = [array for kept, arrived in halves for array in (kept, *arrived)]
    split = 1 + len(halves[0][1])
    inputs = [
        (array, (block, width), lambda i, at, n=n: (jnp.clip(i - n * steps, 0, steps - 1), 0))
        for n, (kept, arrived) in enumerate(halves)
        for array in (kept, *arrived)
    ]
    here = lambda i, at: (i, 0)
    inputs += [
        (cot_rows, (block, width), here),
        (hidden, (block, width), here),
        (inverse, (block, 1), here),
        (gain, (1, width), lambda i, at: (0, 0)),
    ]
    outputs = [(jax.ShapeDtypeStruct((rows, width), kind), (block, width), here) for kind in (F32, BF)]

    def kernel(at_ref, *refs):
        cot_ref, hidden_ref, inv_ref, gain_ref, out_ref, low_ref = refs[len(terms) :]

        def finish(parts):
            value = hidden_ref[...]
            inv = inv_ref[...]
            scaled = gain_ref[...] * add_up(parts)
            mean = jnp.mean(scaled * value, -1, keepdims=True)
            grad = cot_ref[...].astype(F32) + inv * scaled - value * inv**3 * mean
            out_ref[...] = grad
            low_ref[...] = grad.astype(BF)

        @pl.when(pl.program_id(0) < steps)
        def _():
            finish(refs[:split])

        @pl.when(pl.program_id(0) >= steps)
        def _():
            finish(refs[split : len(terms)])

    return small_kernel(kernel, jnp.zeros((1,), jnp.int32), 2 * steps, inputs, outputs)


def plane_gather(values, relay):
    count_a, count_b = (lax.axis_size(axis) for axis in PAIR)
    here_a, here_b, core = (lax.axis_index(axis) for axis in PLANE)
    rows, width = values.shape
    half = rows // 2
    found = {}
    for k in range(count_a):
        found[k, 0] = [(0, shift(values, "da", k))] if k else [(0, values)]
    for k in range(1, count_b):
        found[0, k] = [(0, shift(values, "db", k))]
    for ka in range(1, count_a):
        for kb in range(1, count_b):
            if relay:
                found[ka, kb] = [
                    (0, shift(found[0, kb][0][1][:half], "da", ka)),
                    (half, shift(found[ka, 0][0][1][half:], "db", kb)),
                ]
            else:
                to = [
                    (i // count_b + ka) % count_a * count_b + (i % count_b + kb) % count_b
                    for i in range(count_a * count_b)
                ]
                found[ka, kb] = [(0, lax.ppermute(values, PAIR, list(enumerate(to))))]
    pieces, places = [], []
    for (ka, kb), parts in found.items():
        chip = behind(here_a, ka, count_a) * count_b + behind(here_b, kb, count_b)
        for first, piece in parts:
            other = shift(piece, "core", 1)
            pieces += [(first, piece), (first, other)]
            places += [chip * CORES + core, chip * CORES + 1 - core]
    count = count_a * count_b * CORES
    return gather_blocks(pieces, places, rows, count).reshape(count * rows, width)


def hidden_cuts(total, group, part):
    return [
        (min(j * part, total), max(0, min(part, total - j * part))) for j in range(group)
    ]


def pack_shares(ffn_weight, down_weight, group, part):
    rows, total = down_weight.shape
    cuts = hidden_cuts(total, group, part)

    def kernel(ffn_ref, down_ref, out_ref):
        for j, (first, count) in enumerate(cuts):
            if count < part:
                out_ref[j] = jnp.zeros((rows, 3 * part), BF)
            if count:
                out_ref[j, :, pl.ds(0, count)] = ffn_ref[:, pl.ds(first, count)]
                out_ref[j, :, pl.ds(part, count)] = ffn_ref[:, pl.ds(total + first, count)]
                out_ref[j, :, pl.ds(2 * part, count)] = down_ref[:, pl.ds(first, count)]

    return pl.pallas_call(
        kernel,
        out_shape=jax.ShapeDtypeStruct((group, rows, 3 * part), BF),
        name="pack_shares",
    )(ffn_weight, down_weight)


def unpack_gate_up(summed, ffn_weight, ffn_gain, group, part):
    rows, double = ffn_weight.shape
    total = double // 2
    cuts = hidden_cuts(total, group, part)

    def kernel(sum_ref, weight_ref, gain_ref, out_ref, gain_out_ref):
        gain_sum = jnp.zeros((rows, 1), F32)
        for j, (first, count) in enumerate(cuts):
            if count:
                for source, target in ((0, first), (part, total + first)):
                    piece = sum_ref[j, :, pl.ds(source, count)].astype(F32)
                    out_ref[:, pl.ds(target, count)] = piece
                    weight = weight_ref[:, pl.ds(target, count)].astype(F32)
                    gain_sum = gain_sum + jnp.sum(piece * weight, 1, keepdims=True)
        gain_out_ref[...] = gain_sum / gain_ref[...].astype(F32)

    return pl.pallas_call(
        kernel,
        out_shape=(
            jax.ShapeDtypeStruct((rows, double), F32),
            jax.ShapeDtypeStruct((rows, 1), F32),
        ),
        name="unpack_gate_up",
    )(summed, ffn_weight, ffn_gain[:, None])


def unpack_down(summed, total, group, part):
    rows = summed.shape[1]
    cuts = hidden_cuts(total, group, part)

    def kernel(sum_ref, out_ref):
        for j, (first, count) in enumerate(cuts):
            if count:
                out_ref[:, pl.ds(first, count)] = sum_ref[j, :, pl.ds(0, count)].astype(F32)

    return pl.pallas_call(
        kernel, out_shape=jax.ShapeDtypeStruct((rows, total), F32), name="unpack_down"
    )(summed)


def reorder(values, dp_count, first_count, second_count, halves=(), kind=None):
    rows, width = values.shape
    owned = width // (dp_count * first_count * second_count)
    kind = kind or values.dtype
    half = rows // 2
    terms = [array for kept, arrived in halves for array in (kept, *arrived)]
    split = len(terms) // 2

    def kernel(*refs):
        out_ref = refs[-1]
        for d in range(dp_count):
            for i in range(first_count):
                for j in range(second_count):
                    source = pl.ds(((d * first_count + i) * second_count + j) * owned, owned)
                    target = pl.ds(((d * second_count + j) * first_count + i) * owned, owned)
                    if not terms:
                        out_ref[:, target] = refs[0][:, source].astype(kind)
                        continue
                    for n, start in enumerate((0, half)):
                        piece = refs[0][start : start + half, source]
                        for ref in refs[1:-1][n * split : (n + 1) * split]:
                            piece = piece + ref[:, source].astype(F32)
                        out_ref[start : start + half, target] = piece.astype(kind)

    return pl.pallas_call(
        kernel, out_shape=jax.ShapeDtypeStruct((rows, width), kind), name="reorder"
    )(values, *terms)


def attend(rows_in, kv_pieces, cosine, sine_part, query_pos, key_pos):
    rows = rows_in.shape[0]
    query_scale = HEAD ** (-0.5)
    count = len(kv_pieces)
    length = count * rows

    def kernel(*refs):
        kv_refs = refs[:count]
        q_ref, cos_ref, sin_ref, qp_ref, kp_ref, out_ref, lse_ref, qr_ref, kv_all = refs[count:]
        for i, ref in enumerate(kv_refs):
            kv_all[pl.ds(i * rows, rows), :] = ref[...]
        later = qp_ref[...] - kp_ref[...]
        seen = (later >= 0) & (later < WINDOW)
        lanes = lax.broadcasted_iota(jnp.int32, (rows, LANES), 1)
        totals = jnp.zeros((rows, LANES), F32)
        for h in range(HEADS):
            at = pl.ds(h * HEAD, HEAD)
            rotated = rotate(q_ref[:, at], cos_ref[...], sin_ref[...])
            query = (rotated * query_scale).astype(BF)
            qr_ref[:, at] = query
            scores = jnp.where(seen, contract_cols(query, kv_all[:, :HEAD]), -jnp.inf)
            peak = jnp.max(scores, -1, keepdims=True)
            weights = jnp.exp(scores - peak)
            total = jnp.sum(weights, -1, keepdims=True)
            probs = (weights * (1.0 / total)).astype(BF)
            mixed = jnp.dot(probs, kv_all[:, HEAD:], preferred_element_type=F32)
            out_ref[:, at] = mixed.astype(BF)
            totals = jnp.where(lanes == h, peak + jnp.log(total), totals)
        lse_ref[...] = totals

    return pl.pallas_call(
        kernel,
        out_shape=(
            jax.ShapeDtypeStruct((rows, HEADS * HEAD), BF),
            jax.ShapeDtypeStruct((rows, LANES), F32),
            jax.ShapeDtypeStruct((rows, HEADS * HEAD), BF),
        ),
        scratch_shapes=[pltpu.VMEM((length, 2 * HEAD), BF)],
        cost_estimate=pl.CostEstimate(
            flops=4 * rows * length * HEADS * HEAD,
            transcendentals=rows * length * HEADS,
            bytes_accessed=4 * length * HEAD + 10 * rows * HEADS * HEAD,
        ),
        name="attend",
    )(*kv_pieces, rows_in, cosine, sine_part, query_pos, key_pos)


def attend_back(queries, kv_pieces, cosine, sine_part, query_pos, key_pos, totals, grad_mixed):
    rows = queries.shape[0]
    count = len(kv_pieces)
    length = count * rows
    half = length // 2
    query_scale = HEAD ** (-0.5)

    def kernel(*refs):
        kv_refs = refs[:count]
        q_ref, cos_ref, sin_ref, qp_ref, kp_ref, lse_ref, do_ref = refs[count : count + 7]
        dq_ref, own_ref, other_ref, kv_all, ds_all, probs_all, q_all, do_all = refs[count + 7 :]
        for i, ref in enumerate(kv_refs):
            kv_all[pl.ds(i * rows, rows), :] = ref[...]
        later = qp_ref[...] - kp_ref[...]
        seen = (later >= 0) & (later < WINDOW)
        for h in range(HEADS):
            at = pl.ds(h * HEAD, HEAD)
            below = pl.ds(h * rows, rows)
            query = q_ref[:, at]
            grad_out = do_ref[:, at]
            scores = jnp.where(seen, contract_cols(query, kv_all[:, :HEAD]), -jnp.inf)
            probs = jnp.exp(scores - lse_ref[:, h : h + 1])
            grad_probs = contract_cols(grad_out, kv_all[:, HEAD:])
            delta = jnp.sum(probs * grad_probs, -1, keepdims=True)
            grad_scores = (probs * (grad_probs - delta)).astype(BF)
            ds_all[below, :] = grad_scores
            probs_all[below, :] = probs.astype(BF)
            q_all[below, :] = query
            do_all[below, :] = grad_out
            grad_query = jnp.dot(grad_scores, kv_all[:, :HEAD], preferred_element_type=F32)
            grad_query = unrotate(grad_query, cos_ref[...], sin_ref[...]) * query_scale
            dq_ref[:, at] = grad_query.astype(BF)
        for ref, first, kind in ((own_ref, 0, F32), (other_ref, half, BF)):
            part = pl.ds(first, half)
            ref[:, :HEAD] = contract_rows(ds_all[:, part], q_all[...]).astype(kind)
            ref[:, HEAD:] = contract_rows(probs_all[:, part], do_all[...]).astype(kind)

    stacked = HEADS * rows
    return pl.pallas_call(
        kernel,
        out_shape=(
            jax.ShapeDtypeStruct((rows, HEADS * HEAD), BF),
            jax.ShapeDtypeStruct((half, 2 * HEAD), F32),
            jax.ShapeDtypeStruct((half, 2 * HEAD), BF),
        ),
        scratch_shapes=[
            pltpu.VMEM((length, 2 * HEAD), BF),
            pltpu.VMEM((stacked, length), BF),
            pltpu.VMEM((stacked, length), BF),
            pltpu.VMEM((stacked, HEAD), BF),
            pltpu.VMEM((stacked, HEAD), BF),
        ],
        cost_estimate=pl.CostEstimate(
            flops=10 * rows * length * HEADS * HEAD,
            transcendentals=rows * length * HEADS,
            bytes_accessed=7 * length * HEAD + 10 * rows * HEADS * HEAD,
        ),
        name="attend_back",
    )(*kv_pieces, queries, cosine, sine_part, query_pos, key_pos, totals, grad_mixed)


def plane_specs(dp_count, rows_here):
    together = 2
    steps = dp_count // together

    def tokens(columns):
        return pl.BlockSpec(
            (together, 1, rows_here, columns),
            lambda i, core: (i % steps, jnp.where(i < steps, 1 - core[0], core[0]), 0, 0),
        )

    def halves(columns):
        rows = together * rows_here
        return (
            pl.BlockSpec((rows, columns), lambda i, core: (jnp.minimum(i, steps - 1), 0)),
            pl.BlockSpec((rows, columns), lambda i, core: (jnp.maximum(i - steps, 0), 0)),
        )

    return steps, together * rows_here, tokens, halves


def feed_forward(core, tokens_in, weight, grad_hidden):
    dp_count, _, rows_here, width = tokens_in.shape
    part = grad_hidden.shape[3]
    steps, rows, tokens, halves = plane_specs(dp_count, rows_here)

    def kernel(core_ref, in_ref, weight_ref, grad_ref, hid_ref, dgu_ref, other_ref, own_ref):
        step = pl.program_id(0)
        both = jnp.dot(in_ref[...].reshape(rows, width), weight_ref[...], preferred_element_type=F32)
        gelu_value, gelu_slope = gelu_parts(both[:, :part])
        up_part = both[:, part:]
        grad = grad_ref[...].reshape(rows, part)
        hid_ref[...] = (gelu_value * up_part).astype(BF).reshape(hid_ref.shape)
        dgu = jnp.concatenate([grad * up_part * gelu_slope, grad * gelu_value], 1).astype(BF)
        dgu_ref[...] = dgu.reshape(dgu_ref.shape)
        term = contract_cols(dgu, weight_ref[...]).astype(BF)

        @pl.when(step < steps)
        def _():
            other_ref[...] = term

        @pl.when(step >= steps)
        def _():
            own_ref[...] = term

    count = dp_count * CORES * rows_here
    half = jax.ShapeDtypeStruct((count // 2, width), BF)
    return pl.pallas_call(
        kernel,
        grid_spec=pltpu.PrefetchScalarGridSpec(
            num_scalar_prefetch=1,
            grid=(2 * steps,),
            in_specs=[
                tokens(width),
                pl.BlockSpec((width, 2 * part), lambda i, core: (0, 0)),
                tokens(part),
            ],
            out_specs=(tokens(part), tokens(2 * part), *halves(width)),
        ),
        out_shape=(
            jax.ShapeDtypeStruct((dp_count, CORES, rows_here, part), BF),
            jax.ShapeDtypeStruct((dp_count, CORES, rows_here, 2 * part), BF),
            half,
            half,
        ),
        cost_estimate=pl.CostEstimate(
            flops=8 * count * width * part,
            transcendentals=count * part,
            bytes_accessed=4 * count * width + 4 * width * part + 10 * count * part,
        ),
        name="feed_forward",
    )(core, tokens_in, weight, grad_hidden)


def row_product(left, right):
    tokens, width = left.shape
    columns = right.shape[1]
    block = 256 if tokens % 256 == 0 else tokens

    def kernel(left_ref, right_ref, out_ref):
        out_ref[...] = jnp.dot(left_ref[...], right_ref[...], preferred_element_type=F32)

    return pl.pallas_call(
        kernel,
        grid=(tokens // block,),
        in_specs=[
            pl.BlockSpec((block, width), lambda i: (i, 0)),
            pl.BlockSpec((width, columns), lambda i: (0, 0)),
        ],
        out_specs=pl.BlockSpec((block, columns), lambda i: (i, 0)),
        out_shape=jax.ShapeDtypeStruct((tokens, columns), F32),
        cost_estimate=pl.CostEstimate(
            flops=2 * tokens * width * columns,
            transcendentals=0,
            bytes_accessed=2 * (tokens * width + width * columns) + 4 * tokens * columns,
        ),
        name="row_product",
    )(left, right)


def key_value_grads(own, arrived, cosine, sine_part):
    rows, columns = arrived[0].shape

    def kernel(own_ref, cos_ref, sin_ref, *refs):
        total = own_ref[...]
        for ref in refs[:-1]:
            total = total + ref[...].astype(F32)
        grad_key = unrotate(total[:, :HEAD], cos_ref[...], sin_ref[...])
        refs[-1][...] = jnp.concatenate([grad_key, total[:, HEAD:]], 1).astype(BF)

    return pl.pallas_call(
        kernel, out_shape=jax.ShapeDtypeStruct((rows, columns), BF), name="key_value_grads"
    )(own, cosine, sine_part, *arrived)


def input_grads(grad_query, grad_kv, weight, grad_h, tokens, inverse, gain, counts):
    rows, width_q = grad_query.shape
    width = tokens.shape[1]
    dp_count, z_count = counts
    owned = width // (dp_count * CORES * z_count)

    def kernel(dq_ref, dkv_ref, weight_ref, grad_ref, token_ref, inv_ref, gain_ref, out_ref, row_ref):
        last = width_q + grad_kv.shape[1]
        grad = contract_cols(dq_ref[...], weight_ref[:, :width_q])
        grad = grad + contract_cols(dkv_ref[...], weight_ref[:, width_q:last])
        token = token_ref[...].astype(F32)
        inverse = inv_ref[...]
        scaled = gain_ref[...] * grad
        mean = jnp.mean(scaled * token, -1, keepdims=True)
        row_ref[...] = grad_ref[...] + inverse * scaled - token * inverse**3 * mean
        for d in range(dp_count):
            for c in range(CORES):
                for z in range(z_count):
                    source = pl.ds(((d * CORES + c) * z_count + z) * owned, owned)
                    target = pl.ds(((d * z_count + z) * CORES + c) * owned, owned)
                    out_ref[:, target] = row_ref[:, source]

    return pl.pallas_call(
        kernel,
        out_shape=jax.ShapeDtypeStruct((rows, width), F32),
        scratch_shapes=[pltpu.VMEM((rows, width), F32)],
        cost_estimate=pl.CostEstimate(
            flops=2 * rows * width * (width_q + grad_kv.shape[1]),
            transcendentals=0,
            bytes_accessed=2 * width * weight.shape[1] + 10 * rows * width,
        ),
        name="input_grads",
    )(grad_query, grad_kv, weight, grad_h, tokens, inverse, gain)


def down_product(core, hidden, weight):
    dp_count, _, rows_here, part = hidden.shape
    width = weight.shape[0]
    steps, rows, tokens, halves = plane_specs(dp_count, rows_here)

    def kernel(core_ref, in_ref, weight_ref, other_ref, own_ref):
        step = pl.program_id(0)
        term = contract_cols(in_ref[...].reshape(rows, part), weight_ref[...]).astype(BF)

        @pl.when(step < steps)
        def _():
            other_ref[...] = term

        @pl.when(step >= steps)
        def _():
            own_ref[...] = term

    count = dp_count * CORES * rows_here
    half = jax.ShapeDtypeStruct((count // 2, width), BF)
    return pl.pallas_call(
        kernel,
        grid_spec=pltpu.PrefetchScalarGridSpec(
            num_scalar_prefetch=1,
            grid=(2 * steps,),
            in_specs=[tokens(part), pl.BlockSpec((width, part), lambda i, core: (0, 0))],
            out_specs=halves(width),
        ),
        out_shape=(half, half),
        cost_estimate=pl.CostEstimate(
            flops=2 * count * width * part,
            transcendentals=0,
            bytes_accessed=2 * count * (width + part) + 2 * width * part,
        ),
        name="down_product",
    )(core, hidden, weight)


def weight_term(left, right, dp_count, z_count):
    tokens, width = left.shape
    columns = right.shape[1]
    per_dp = width // dp_count
    owned = per_dp // (z_count * CORES)
    together = 1
    while (together * per_dp) % LANES:
        together *= 2
    block = together * per_dp

    def kernel(left_ref, right_ref, out_ref):
        term = contract_rows(left_ref[...], right_ref[...]).astype(BF)
        for d in range(together):
            for c in range(CORES):
                for z in range(z_count):
                    first = d * per_dp + (c * z_count + z) * owned
                    out_ref[z, d, c] = term[first : first + owned]

    return pl.pallas_call(
        kernel,
        grid=(width // block,),
        in_specs=[
            pl.BlockSpec((tokens, block), lambda i: (0, i)),
            pl.BlockSpec((tokens, columns), lambda i: (0, 0)),
        ],
        out_specs=pl.BlockSpec(
            (z_count, together, CORES, owned, columns), lambda i: (0, i, 0, 0, 0)
        ),
        out_shape=jax.ShapeDtypeStruct((z_count, dp_count, CORES, owned, columns), BF),
        cost_estimate=pl.CostEstimate(
            flops=2 * tokens * width * columns,
            transcendentals=0,
            bytes_accessed=2 * (tokens * width + tokens * columns + width * columns),
        ),
        name="weight_term",
    )(left, right)


def body(
    block_input, qkv_weight, out_weight, ffn_weight, down_weight, attn_gain, ffn_gain, cotangent
):
    tokens = block_input[0]
    cot_rows = cotangent[0]
    rows_here, width = tokens.shape
    owned_rows = qkv_weight.shape[0]
    dp_count = lax.axis_size("da") * lax.axis_size("db")
    z_count = lax.axis_size("z")
    z_index = lax.axis_index("z")
    core = lax.axis_index("core")
    group = dp_count * CORES
    width_q = HEADS * HEAD
    width_qkv = width_q + 2 * HEAD
    part = -(-FF // (LANES * group)) * LANES

    tokens = reorder(tokens, dp_count, z_count, CORES)
    cot_rows = reorder(cot_rows, dp_count, z_count, CORES)

    gain_columns = jnp.stack([attn_gain, ffn_gain], 1)
    gain_columns = jnp.pad(gain_columns, ((0, 0), (0, LANES - 2)))
    qkv_line = gather(jnp.concatenate([qkv_weight, gain_columns], 1), "z")
    packed = pack_shares(ffn_weight, down_weight, group, part)
    mine = exchange(packed, PLANE)
    qkv_line, mine, out_weight = lax.optimization_barrier((qkv_line, mine, out_weight))
    down_mine, gate_up_mine = mine[..., 2 * part :], mine[..., : 2 * part]
    down_lines = line_gather(down_mine, "z")
    gate_up_lines = line_gather(gate_up_mine, "z")
    down_w = place_line(z_index, z_count, down_mine, *down_lines)
    gate_up_w = place_line(z_index, z_count, gate_up_mine, *gate_up_lines)
    qkv_gain = gather(qkv_line, PLANE)
    qkv_full = qkv_gain[:, :width_qkv]
    gain_one = qkv_gain[:, width_qkv].astype(F32)
    gain_two = qkv_gain[:, width_qkv + 1].astype(F32)
    out_pieces = [out_weight] + [shift(out_weight, "z", k) for k in range(1, z_count)]
    out_places = [behind(z_index, k, z_count) for k in range(z_count)]
    out_pieces = [(0, piece) for piece in out_pieces]
    out_line = gather_blocks(out_pieces, out_places, owned_rows, z_count)
    out_line = out_line.reshape(z_count * owned_rows, width_q)
    out_full = plane_gather(out_line, False)
    cot_plane = plane_gather(cot_rows, True)

    positions = (z_index * CORES + core) * rows_here + jnp.arange(rows_here, dtype=jnp.int32)
    cosine, sine_part = rope_tables(positions)
    token_f = tokens.astype(jnp.float32)
    inv_one = lax.rsqrt(jnp.mean(token_f * token_f, -1, keepdims=True) + EPSILON)
    normed_one = (token_f * inv_one * gain_one).astype(jnp.bfloat16)
    qkv_rows = jnp.dot(normed_one, qkv_full, preferred_element_type=jnp.float32)
    keys_own = rotate(qkv_rows[:, width_q : width_q + HEAD], cosine, sine_part).astype(jnp.bfloat16)
    kv_rows = jnp.concatenate([keys_own, qkv_rows[:, width_q + HEAD :].astype(jnp.bfloat16)], -1)
    kv_pieces = [kv_rows] + [shift(kv_rows, "z", k) for k in range(1, z_count)]
    kv_pieces = kv_pieces + [shift(piece, "core", 1) for piece in kv_pieces]
    block_z = lax.rem(z_index + z_count - jnp.arange(z_count, dtype=jnp.int32), z_count)
    block_at = jnp.concatenate([block_z * CORES + core, block_z * CORES + (1 - core)])
    key_pos = (
        block_at[:, None] * rows_here + jnp.arange(rows_here, dtype=jnp.int32)[None, :]
    ).reshape(1, -1)
    query_pos = positions[:, None]
    attn_flat, log_total, queries = attend(
        qkv_rows, kv_pieces, cosine, sine_part, query_pos, key_pos
    )
    hidden_one = token_f + contract_cols(attn_flat, out_full)
    inv_two = lax.rsqrt(jnp.mean(hidden_one * hidden_one, -1, keepdims=True) + EPSILON)
    normed_two = (hidden_one * inv_two * gain_two).astype(jnp.bfloat16)

    normed_plane = gather(normed_two, PLANE)
    grad_hidden = row_product(cot_plane, down_w)
    core_at = jnp.full((1,), core, jnp.int32)
    at = jnp.stack([lax.axis_index(axis) for axis in ("da", "db", "core", "z")]).astype(jnp.int32)
    in_blocks = (dp_count, CORES, rows_here, -1)
    hidden, grad_gate_up, dn2_other, dn2_own = feed_forward(
        core_at, normed_plane.reshape(in_blocks), gate_up_w, grad_hidden.reshape(in_blocks)
    )
    dn2_halves = reduce_tokens(dn2_own, dn2_other, None)
    down_other, down_own = down_product(core_at, hidden, down_w)
    down_halves = reduce_tokens(down_own, down_other, at)
    output_rows = reorder(hidden_one, dp_count, CORES, z_count, down_halves, BF)

    def sum_ffn(left, right):
        right = right.reshape(left.shape[0], -1)
        term = weight_term(left, right, dp_count, z_count).reshape(width, right.shape[1])
        return scatter(term, "z").reshape(group, owned_rows, right.shape[1])

    gate_up_sum = sum_ffn(normed_plane, grad_gate_up)
    gate_up_sum = exchange(gate_up_sum, PLANE)
    down_sum = sum_ffn(cot_plane, hidden)
    down_sum, gate_up_sum = lax.optimization_barrier((down_sum, gate_up_sum))
    down_sum = exchange(down_sum, PLANE)
    grad_ffn, gain_two_grad = unpack_gate_up(gate_up_sum, ffn_weight, ffn_gain, group, part)
    gain_two_grad = gain_two_grad[:, 0]
    grad_down = unpack_down(down_sum, FF, group, part)

    grad_h_one, grad_h_bf = hidden_grads(dn2_halves, cot_rows, hidden_one, inv_two, gain_two[None])
    grad_attn = jnp.dot(grad_h_bf, out_full, preferred_element_type=F32).astype(BF)
    grad_query, kv_own, kv_other = attend_back(
        queries, kv_pieces, cosine, sine_part, query_pos, key_pos, log_total, grad_attn
    )
    kv_other = shift(kv_other, "core", 1)
    paired = (kv_own + kv_other.astype(F32)).reshape(z_count, rows_here, 2 * HEAD)
    arrived = []
    for k in range(1, z_count):
        piece = paired[k].astype(BF)
        arrived.append(shift(piece, "z", -k))
    grad_kv = key_value_grads(paired[0], arrived, cosine, sine_part)

    grad_rows = input_grads(
        grad_query, grad_kv, qkv_gain, grad_h_one, tokens, inv_one, gain_one[None], (dp_count, z_count)
    )

    out_halves = reduce_term(grad_h_bf, attn_flat, at)
    query_halves = reduce_term(normed_one, grad_query, None)
    kv_halves = reduce_term(normed_one, grad_kv, None)
    out_terms = reduce_line([out_halves], at, owned_rows)
    qkv_terms = reduce_line([query_halves, kv_halves], at, owned_rows)
    grad_out, grad_qkv, gain_one_grad = attention_weight_grads(
        out_terms, qkv_terms, qkv_weight, attn_gain
    )
    gain_one_grad = gain_one_grad[:, 0]
    return (
        output_rows[None],
        grad_rows[None],
        grad_qkv,
        grad_out,
        grad_ffn,
        grad_down,
        gain_one_grad,
        gain_two_grad,
    )


def solution(mesh):
    dp_count = mesh.shape["dp"]
    seq_count = mesh.shape["seq"]
    split = Mesh(mesh.devices.reshape(dp_count // 2, 2, seq_count // CORES, CORES), EVERY)
    by_token = P(PAIR, SEQ, None)
    by_row = P(EVERY, None)
    by_gain = P(EVERY)


    return jax.shard_map(
        body,
        mesh=split,
        in_specs=(by_token, by_row, by_row, by_row, by_row, by_gain, by_gain, by_token),
        out_specs=(by_token, by_token, by_row, by_row, by_row, by_row, by_gain, by_gain),
        check_vma=False,
    )
```

```python
import jax
import jax.numpy as jnp
from jax import lax
from jax.experimental import pallas as pl
from jax.experimental.pallas import tpu as pltpu
from jax.sharding import Mesh, PartitionSpec as P


HEADS = 5
HEAD = 256
FF = 3840
WINDOW = 2048


EPSILON = 1e-06
GELU_C = 0.7978845608028654
CORES = 2
EVERY = ("da", "db", "z", "core")
SEQ = ("z", "core")
PAIR = ("da", "db")
PLANE = ("da", "db", "core")
LANES = 128
BF = jnp.bfloat16
F32 = jnp.float32


def rope_tables(positions):
    half_dim = HEAD // 2
    frequency = 10000.0 ** (-jnp.arange(half_dim, dtype=jnp.float32) / half_dim)
    angles = positions.astype(jnp.float32)[:, None] * frequency[None, :]
    return (jnp.cos(angles), jnp.sin(angles))


def rotate(values, cosine, sine_part):
    half_dim = values.shape[-1] // 2
    first_half = values[..., :half_dim]
    second_half = values[..., half_dim:]
    return jnp.concatenate(
        [
            first_half * cosine - second_half * sine_part,
            second_half * cosine + first_half * sine_part,
        ],
        -1,
    )


def unrotate(values, cosine, sine_part):
    half_dim = values.shape[-1] // 2
    first_half = values[..., :half_dim]
    second_half = values[..., half_dim:]
    return jnp.concatenate(
        [
            first_half * cosine + second_half * sine_part,
            second_half * cosine - first_half * sine_part,
        ],
        -1,
    )


def gelu_parts(gate_in):
    cubic_term = 0.044715
    inner_arg = GELU_C * (gate_in + cubic_term * gate_in**3)
    tangent = jnp.tanh(inner_arg)
    gelu_value = 0.5 * gate_in * (1.0 + tangent)
    gelu_slope = 0.5 * (1.0 + tangent) + 0.5 * gate_in * (1.0 - tangent**2) * GELU_C * (
        1.0 + 3.0 * cubic_term * gate_in**2
    )
    return (gelu_value, gelu_slope)


def contract_rows(left_rows, right_rows):
    return lax.dot_general(
        left_rows, right_rows, (((0,), (0,)), ((), ())), preferred_element_type=jnp.float32
    )


def contract_cols(left_rows, right_rows):
    return lax.dot_general(
        left_rows, right_rows, (((1,), (1,)), ((), ())), preferred_element_type=jnp.float32
    )


def gather(values, axes, axis=0, tiled=True):
    return lax.all_gather(values, axes, axis=axis, tiled=tiled)


def scatter(values, axes, axis=0):
    return lax.psum_scatter(values, axes, scatter_dimension=axis, tiled=True)


def exchange(values, axes):
    return lax.all_to_all(values, axes, split_axis=0, concat_axis=0, tiled=True)


def shift(values, axis, step):
    count = lax.axis_size(axis)
    return lax.ppermute(values, axis, [(i, (i + step) % count) for i in range(count)])


def slide(values, axis, step):
    count = lax.axis_size(axis)
    pairs = [(i, i + step) for i in range(count) if 0 <= i + step < count]
    return lax.ppermute(values, axis, pairs)


def pick(values, index, axis):
    return lax.dynamic_index_in_dim(values, index, axis, False, allow_negative_indices=False)


def behind(here, step, count):
    return lax.rem(here + (count - step) % count, count)


def line_gather(values, axis):
    right, left = values, values
    rights, lefts = [], []
    for _ in range(1, lax.axis_size(axis)):
        right = slide(right, axis, 1)
        left = slide(left, axis, -1)
        rights.append(right)
        lefts.append(left)
    return rights, lefts


def gather_blocks(pieces, places, rows, count):
    firsts, pieces = zip(*pieces)
    columns = pieces[0].shape[1]
    block = columns
    while block % (2 * LANES) == 0 and block > 1024:
        block //= 2

    def kernel(places_ref, *refs):
        for k, first in enumerate(firsts):
            refs[-1][places_ref[k], pl.ds(first, pieces[k].shape[0])] = refs[k][...]

    return pl.pallas_call(
        kernel,
        grid_spec=pltpu.PrefetchScalarGridSpec(
            num_scalar_prefetch=1,
            grid=(columns // block,),
            in_specs=[
                pl.BlockSpec((piece.shape[0], block), lambda i, at: (0, i)) for piece in pieces
            ],
            out_specs=pl.BlockSpec((count, rows, block), lambda i, at: (0, 0, i)),
        ),
        out_shape=jax.ShapeDtypeStruct((count, rows, columns), pieces[0].dtype),
        cost_estimate=pl.CostEstimate(
            flops=0, transcendentals=0, bytes_accessed=4 * count * rows * columns
        ),
        name="gather_blocks",
    )(jnp.stack(places).astype(jnp.int32), *pieces)


def place_line(z_index, z_count, mine, rights, lefts):
    group, owned, columns = mine.shape
    together = 2

    def kernel(z_ref, mine_ref, *refs):
        out_ref = refs[-1]
        z = z_ref[0]
        out_ref[:, z] = mine_ref[...]
        for k in range(1, z_count):

            @pl.when(z >= k)
            def _():
                out_ref[:, z - k] = refs[k - 1][...]

            @pl.when(z + k < z_count)
            def _():
                out_ref[:, z + k] = refs[z_count + k - 2][...]

    piece = pl.BlockSpec((together, owned, columns), lambda i, z: (i, 0, 0))
    placed = pl.pallas_call(
        kernel,
        grid_spec=pltpu.PrefetchScalarGridSpec(
            num_scalar_prefetch=1,
            grid=(group // together,),
            in_specs=[piece] * (2 * z_count - 1),
            out_specs=pl.BlockSpec(
                (together, z_count, owned, columns), lambda i, z: (i, 0, 0, 0)
            ),
        ),
        out_shape=jax.ShapeDtypeStruct((group, z_count, owned, columns), BF),
        cost_estimate=pl.CostEstimate(
            flops=0, transcendentals=0, bytes_accessed=6 * z_count * group * owned * columns
        ),
        name="place_line",
    )(jnp.full((1,), z_index, jnp.int32), mine, *rights, *lefts)
    return placed.reshape(group * z_count * owned, columns)


def split_rows(rows, row_bytes):
    best = rows
    for block in range(16, rows, 16):
        if rows % block == 0 and block * row_bytes > 3 << 20:
            return block
    return best


def small_kernel(kernel, at, grid, inputs, outputs):
    moved = sum(array.size * array.dtype.itemsize for array, _, _ in (*inputs, *outputs))
    return pl.pallas_call(
        kernel,
        grid_spec=pltpu.PrefetchScalarGridSpec(
            num_scalar_prefetch=1,
            grid=(grid,),
            in_specs=[pl.BlockSpec(block, index) for _, block, index in inputs],
            out_specs=[pl.BlockSpec(block, index) for _, block, index in outputs],
        ),
        out_shape=[shape for shape, _, _ in outputs],
        cost_estimate=pl.CostEstimate(flops=0, transcendentals=0, bytes_accessed=moved),
    )(at, *(array for array, _, _ in inputs))


def pair_split(owns, other, at, which):
    count_a, count_b, rows, columns = other.shape
    half = rows // 2
    block = split_rows(half, 12 * count_a * count_b * columns)
    steps = half // block

    def kernel(at_ref, *refs):
        a, b = at_ref[0], at_ref[1]
        mine, (other_0, other_1), outs = refs[: 2 * len(owns)], refs[2 * len(owns) :][:2], refs[2 * len(owns) + 2 :]
        first = 0
        for n, own in enumerate(owns):
            at_columns = pl.ds(first, own.shape[-1])
            first += own.shape[-1]
            own_0, own_1 = mine[2 * n : 2 * n + 2]
            for k in range(count_b):
                j = lax.rem(b + k, count_b)
                total = own_0[:, j, 0].astype(F32) + other_0[:, j, :, at_columns].astype(F32)
                outs[k][:, :, at_columns] = total.astype(BF)
            for k in range(count_a):
                i = lax.rem(a + k, count_a)
                total = own_1[i, :, 0].astype(F32) + other_1[i, :, :, at_columns].astype(F32)
                outs[count_b + k][:, :, at_columns] = total.astype(BF)

    inputs = [
        (own, (count_a, count_b, 1, block, own.shape[-1]), index)
        for own in owns
        for index in (
            lambda i, at: (0, 0, at[2] if which else 0, i, 0),
            lambda i, at: (0, 0, at[2] if which else 0, i + steps, 0),
        )
    ]
    inputs += [
        (other, (count_a, count_b, block, columns), index)
        for index in (lambda i, at: (0, 0, i, 0), lambda i, at: (0, 0, i + steps, 0))
    ]
    outputs = [
        (
            jax.ShapeDtypeStruct((count, half, columns), BF),
            (count, block, columns),
            lambda i, at: (0, i, 0),
        )
        for count in (count_a,) * count_b + (count_b,) * count_a
    ]
    outs = small_kernel(kernel, at, steps, inputs, outputs)
    return outs[:count_b], outs[count_b:]


def sum_split(kept, arrived, at, axes):
    inputs, outputs = [], []
    for keep, pieces in zip(kept, arrived):
        count, half, columns = keep.shape
        block = split_rows(half, 12 * count * columns)
        for array in (keep, *pieces):
            inputs.append((array, (count, block, columns), lambda i, at: (0, i, 0)))
        for k in range(count):
            shape = jax.ShapeDtypeStruct((half, columns), BF if k else F32)
            outputs.append((shape, (block, columns), lambda i, at: (i, 0)))
    counts = [keep.shape[0] for keep in kept]

    def kernel(at_ref, *refs):
        ins, outs = list(refs[: len(inputs)]), list(refs[len(inputs) :])
        for count, pieces, axis in zip(counts, arrived, axes):
            mine = [ins.pop(0) for _ in range(1 + len(pieces))]
            for k in range(count):
                i = lax.rem(at_ref[axis] + k, count)
                total = mine[0][i].astype(F32)
                for ref in mine[1:]:
                    total = total + ref[i].astype(F32)
                out = outs.pop(0)
                out[...] = total.astype(out.dtype)

    outs = small_kernel(kernel, at, half // block, inputs, outputs)
    return (outs[0], outs[1 : counts[0]]), (outs[counts[0]], outs[counts[0] + 1 :])


def reduce_plane(owns, other, at, which):
    other = shift(other, "core", 1)
    first, second = pair_split(owns, other, at, which)
    arrived = (
        [shift(piece, "db", k + 1) for k, piece in enumerate(first[1:])],
        [shift(piece, "da", k + 1) for k, piece in enumerate(second[1:])],
    )
    (kept_0, sends_0), (kept_1, sends_1) = sum_split((first[0], second[0]), arrived, at, (0, 1))
    arrived_0 = [shift(piece, "da", k + 1) for k, piece in enumerate(sends_0)]
    arrived_1 = [shift(piece, "db", k + 1) for k, piece in enumerate(sends_1)]
    return (kept_0, arrived_0), (kept_1, arrived_1)


def sum_axis(values, axis, dim):
    kept, arrived = send_axis(values, axis, dim)
    for piece in arrived:
        kept = kept + piece.astype(F32)
    return kept


def send_axis(values, axis, dim):
    count = lax.axis_size(axis)
    here = lax.axis_index(axis)
    kept = pick(values, here, dim).astype(F32)
    pieces = [pick(values, behind(here, -k, count), dim).astype(BF) for k in range(1, count)]
    return kept, [shift(piece, axis, k + 1) for k, piece in enumerate(pieces)]


def reduce_plane_fused(own, other):
    other = shift(other, "core", 1)
    paired = (own.astype(F32) + other.astype(F32)).astype(BF)
    half = own.shape[2] // 2
    first = sum_axis(paired[:, :, :half], "db", 1)
    second = sum_axis(paired[:, :, half:], "da", 0)
    return send_axis(first, "da", 0), send_axis(second, "db", 0)


def add_up(refs):
    total = refs[0][...].astype(F32)
    for ref in refs[1:]:
        total = total + ref[...].astype(F32)
    return total


def reduce_tokens(own, other, at):
    count_a, count_b = (lax.axis_size(axis) for axis in PAIR)
    own, other = (x.reshape(count_a, count_b, -1, x.shape[1]) for x in (own, other))
    if at is None:
        return reduce_plane_fused(own, other)
    return reduce_plane((own[:, :, None],), other, at, 0)


def reduce_term(left, right, at):
    count_a, count_b = (lax.axis_size(axis) for axis in PAIR)
    term = contract_rows(left, right).astype(BF)
    term = term.reshape(count_a, count_b, CORES, -1, right.shape[1])
    core = lax.axis_index("core")
    other = pick(term, 1 - core, 2)
    if at is None:
        return reduce_plane_fused(pick(term, core, 2), other)
    return reduce_plane((term,), other, at, 2)


def reduce_line(terms, at, owned):
    count_z = lax.axis_size("z")
    middle = count_z // 2
    widths = [halves[0][0].shape[-1] for halves in terms]
    columns = sum(widths)
    arrays = [
        array.reshape(middle, owned, -1)
        for halves in terms
        for kept, arrived in halves
        for array in (kept, *arrived)
    ]
    splits = [1 + len(arrived) for halves in terms for _, arrived in halves]

    def kernel(at_ref, *refs):
        ins, outs, all_rows = list(refs[: len(arrays)]), refs[len(arrays) : -1], refs[-1]
        first = 0
        for n, size in enumerate(splits):
            width = widths[n // 2]
            start = middle * (n % 2)
            all_rows[start : start + middle, :, first : first + width] = add_up(ins[:size])
            ins = ins[size:]
            first += width * (n % 2)
        for k in range(count_z):
            outs[k][...] = all_rows[lax.rem(at_ref[3] + k, count_z)].astype(outs[k].dtype)

    kept, *sends = pl.pallas_call(
        kernel,
        grid_spec=pltpu.PrefetchScalarGridSpec(
            num_scalar_prefetch=1,
            grid=(1,),
            in_specs=[pl.BlockSpec(array.shape, lambda i, at: (0, 0, 0)) for array in arrays],
            out_specs=[pl.BlockSpec((owned, columns), lambda i, at: (0, 0))] * count_z,
            scratch_shapes=[pltpu.VMEM((count_z, owned, columns), F32)],
        ),
        out_shape=[
            jax.ShapeDtypeStruct((owned, columns), BF if k else F32) for k in range(count_z)
        ],
        name="row_split",
    )(at, *arrays)
    arrived = [shift(piece, "z", k + 1) for k, piece in enumerate(sends)]
    return [kept, *arrived]


def attention_weight_grads(terms, qkv_weight, attn_gain):
    rows, width_qkv = qkv_weight.shape
    width_out = terms[0].shape[1] - width_qkv
    count = len(terms)

    def kernel(*refs):
        weight_ref, gain_ref, out_ref, qkv_ref, gain_out_ref = refs[count:]
        total = add_up(refs[:count])
        out_ref[...] = total[:, :width_out]
        grad = total[:, width_out:]
        qkv_ref[...] = grad
        gain_sum = jnp.sum(grad * weight_ref[...].astype(F32), 1, keepdims=True)
        gain_out_ref[...] = gain_sum / gain_ref[...].astype(F32)

    return pl.pallas_call(
        kernel,
        out_shape=(
            jax.ShapeDtypeStruct((rows, width_out), F32),
            jax.ShapeDtypeStruct((rows, width_qkv), F32),
            jax.ShapeDtypeStruct((rows, 1), F32),
        ),
        name="attention_weight_grads",
    )(*terms, qkv_weight, attn_gain[:, None])


def hidden_grads(halves, cot_rows, hidden, inverse, gain):
    rows, width = cot_rows.shape
    half = rows // 2
    block = split_rows(half, 20 * width)
    steps = half // block
    terms = [array for kept, arrived in halves for array in (kept, *arrived)]
    split = 1 + len(halves[0][1])
    inputs = [
        (array, (block, width), lambda i, at, n=n: (jnp.clip(i - n * steps, 0, steps - 1), 0))
        for n, (kept, arrived) in enumerate(halves)
        for array in (kept, *arrived)
    ]
    here = lambda i, at: (i, 0)
    inputs += [
        (cot_rows, (block, width), here),
        (hidden, (block, width), here),
        (inverse, (block, 1), here),
        (gain, (1, width), lambda i, at: (0, 0)),
    ]
    outputs = [(jax.ShapeDtypeStruct((rows, width), kind), (block, width), here) for kind in (F32, BF)]

    def kernel(at_ref, *refs):
        cot_ref, hidden_ref, inv_ref, gain_ref, out_ref, low_ref = refs[len(terms) :]

        def finish(parts):
            value = hidden_ref[...]
            inv = inv_ref[...]
            scaled = gain_ref[...] * add_up(parts)
            mean = jnp.mean(scaled * value, -1, keepdims=True)
            grad = cot_ref[...].astype(F32) + inv * scaled - value * inv**3 * mean
            out_ref[...] = grad
            low_ref[...] = grad.astype(BF)

        @pl.when(pl.program_id(0) < steps)
        def _():
            finish(refs[:split])

        @pl.when(pl.program_id(0) >= steps)
        def _():
            finish(refs[split : len(terms)])

    return small_kernel(kernel, jnp.zeros((1,), jnp.int32), 2 * steps, inputs, outputs)


def plane_gather(values, relay):
    count_a, count_b = (lax.axis_size(axis) for axis in PAIR)
    here_a, here_b, core = (lax.axis_index(axis) for axis in PLANE)
    rows, width = values.shape
    half = rows // 2
    found = {}
    for k in range(count_a):
        found[k, 0] = [(0, shift(values, "da", k))] if k else [(0, values)]
    for k in range(1, count_b):
        found[0, k] = [(0, shift(values, "db", k))]
    for ka in range(1, count_a):
        for kb in range(1, count_b):
            if relay:
                found[ka, kb] = [
                    (0, shift(found[0, kb][0][1][:half], "da", ka)),
                    (half, shift(found[ka, 0][0][1][half:], "db", kb)),
                ]
            else:
                to = [
                    (i // count_b + ka) % count_a * count_b + (i % count_b + kb) % count_b
                    for i in range(count_a * count_b)
                ]
                found[ka, kb] = [(0, lax.ppermute(values, PAIR, list(enumerate(to))))]
    pieces, places = [], []
    for (ka, kb), parts in found.items():
        chip = behind(here_a, ka, count_a) * count_b + behind(here_b, kb, count_b)
        for first, piece in parts:
            other = shift(piece, "core", 1)
            pieces += [(first, piece), (first, other)]
            places += [chip * CORES + core, chip * CORES + 1 - core]
    count = count_a * count_b * CORES
    return gather_blocks(pieces, places, rows, count).reshape(count * rows, width)


def hidden_cuts(total, group, part):
    return [
        (min(j * part, total), max(0, min(part, total - j * part))) for j in range(group)
    ]


def pack_shares(ffn_weight, down_weight, group, part):
    rows, total = down_weight.shape
    cuts = hidden_cuts(total, group, part)

    def kernel(ffn_ref, down_ref, out_ref):
        for j, (first, count) in enumerate(cuts):
            if count < part:
                out_ref[j] = jnp.zeros((rows, 3 * part), BF)
            if count:
                out_ref[j, :, pl.ds(0, count)] = ffn_ref[:, pl.ds(first, count)]
                out_ref[j, :, pl.ds(part, count)] = ffn_ref[:, pl.ds(total + first, count)]
                out_ref[j, :, pl.ds(2 * part, count)] = down_ref[:, pl.ds(first, count)]

    return pl.pallas_call(
        kernel,
        out_shape=jax.ShapeDtypeStruct((group, rows, 3 * part), BF),
        name="pack_shares",
    )(ffn_weight, down_weight)


def unpack_gate_up(summed, ffn_weight, ffn_gain, group, part):
    rows, double = ffn_weight.shape
    total = double // 2
    cuts = hidden_cuts(total, group, part)

    def kernel(sum_ref, weight_ref, gain_ref, out_ref, gain_out_ref):
        gain_sum = jnp.zeros((rows, 1), F32)
        for j, (first, count) in enumerate(cuts):
            if count:
                for source, target in ((0, first), (part, total + first)):
                    piece = sum_ref[j, :, pl.ds(source, count)].astype(F32)
                    out_ref[:, pl.ds(target, count)] = piece
                    weight = weight_ref[:, pl.ds(target, count)].astype(F32)
                    gain_sum = gain_sum + jnp.sum(piece * weight, 1, keepdims=True)
        gain_out_ref[...] = gain_sum / gain_ref[...].astype(F32)

    return pl.pallas_call(
        kernel,
        out_shape=(
            jax.ShapeDtypeStruct((rows, double), F32),
            jax.ShapeDtypeStruct((rows, 1), F32),
        ),
        name="unpack_gate_up",
    )(summed, ffn_weight, ffn_gain[:, None])


def unpack_down(summed, total, group, part):
    rows = summed.shape[1]
    cuts = hidden_cuts(total, group, part)

    def kernel(sum_ref, out_ref):
        for j, (first, count) in enumerate(cuts):
            if count:
                out_ref[:, pl.ds(first, count)] = sum_ref[j, :, pl.ds(0, count)].astype(F32)

    return pl.pallas_call(
        kernel, out_shape=jax.ShapeDtypeStruct((rows, total), F32), name="unpack_down"
    )(summed)


def reorder(values, dp_count, first_count, second_count, halves=(), kind=None):
    rows, width = values.shape
    owned = width // (dp_count * first_count * second_count)
    kind = kind or values.dtype
    half = rows // 2
    terms = [array for kept, arrived in halves for array in (kept, *arrived)]
    split = len(terms) // 2

    def kernel(*refs):
        out_ref = refs[-1]
        for d in range(dp_count):
            for i in range(first_count):
                for j in range(second_count):
                    source = pl.ds(((d * first_count + i) * second_count + j) * owned, owned)
                    target = pl.ds(((d * second_count + j) * first_count + i) * owned, owned)
                    if not terms:
                        out_ref[:, target] = refs[0][:, source].astype(kind)
                        continue
                    for n, start in enumerate((0, half)):
                        piece = refs[0][start : start + half, source]
                        for ref in refs[1:-1][n * split : (n + 1) * split]:
                            piece = piece + ref[:, source].astype(F32)
                        out_ref[start : start + half, target] = piece.astype(kind)

    return pl.pallas_call(
        kernel, out_shape=jax.ShapeDtypeStruct((rows, width), kind), name="reorder"
    )(values, *terms)


def attend(rows_in, kv_pieces, cosine, sine_part, query_pos, key_pos):
    rows = rows_in.shape[0]
    query_scale = HEAD ** (-0.5)
    count = len(kv_pieces)
    length = count * rows

    def kernel(*refs):
        kv_refs = refs[:count]
        q_ref, cos_ref, sin_ref, qp_ref, kp_ref, out_ref, lse_ref, qr_ref, kv_all = refs[count:]
        for i, ref in enumerate(kv_refs):
            kv_all[pl.ds(i * rows, rows), :] = ref[...]
        later = qp_ref[...] - kp_ref[...]
        seen = (later >= 0) & (later < WINDOW)
        lanes = lax.broadcasted_iota(jnp.int32, (rows, LANES), 1)
        totals = jnp.zeros((rows, LANES), F32)
        for h in range(HEADS):
            at = pl.ds(h * HEAD, HEAD)
            rotated = rotate(q_ref[:, at], cos_ref[...], sin_ref[...])
            query = (rotated * query_scale).astype(BF)
            qr_ref[:, at] = query
            scores = jnp.where(seen, contract_cols(query, kv_all[:, :HEAD]), -jnp.inf)
            peak = jnp.max(scores, -1, keepdims=True)
            weights = jnp.exp(scores - peak)
            total = jnp.sum(weights, -1, keepdims=True)
            probs = (weights * (1.0 / total)).astype(BF)
            mixed = jnp.dot(probs, kv_all[:, HEAD:], preferred_element_type=F32)
            out_ref[:, at] = mixed.astype(BF)
            totals = jnp.where(lanes == h, peak + jnp.log(total), totals)
        lse_ref[...] = totals

    return pl.pallas_call(
        kernel,
        out_shape=(
            jax.ShapeDtypeStruct((rows, HEADS * HEAD), BF),
            jax.ShapeDtypeStruct((rows, LANES), F32),
            jax.ShapeDtypeStruct((rows, HEADS * HEAD), BF),
        ),
        scratch_shapes=[pltpu.VMEM((length, 2 * HEAD), BF)],
        cost_estimate=pl.CostEstimate(
            flops=4 * rows * length * HEADS * HEAD,
            transcendentals=rows * length * HEADS,
            bytes_accessed=4 * length * HEAD + 10 * rows * HEADS * HEAD,
        ),
        name="attend",
    )(*kv_pieces, rows_in, cosine, sine_part, query_pos, key_pos)


def attend_back(queries, kv_pieces, cosine, sine_part, query_pos, key_pos, totals, grad_mixed):
    rows = queries.shape[0]
    count = len(kv_pieces)
    length = count * rows
    half = length // 2
    query_scale = HEAD ** (-0.5)

    def kernel(*refs):
        kv_refs = refs[:count]
        q_ref, cos_ref, sin_ref, qp_ref, kp_ref, lse_ref, do_ref = refs[count : count + 7]
        dq_ref, own_ref, other_ref, kv_all, ds_all, probs_all, q_all, do_all = refs[count + 7 :]
        for i, ref in enumerate(kv_refs):
            kv_all[pl.ds(i * rows, rows), :] = ref[...]
        later = qp_ref[...] - kp_ref[...]
        seen = (later >= 0) & (later < WINDOW)
        for h in range(HEADS):
            at = pl.ds(h * HEAD, HEAD)
            below = pl.ds(h * rows, rows)
            query = q_ref[:, at]
            grad_out = do_ref[:, at]
            scores = jnp.where(seen, contract_cols(query, kv_all[:, :HEAD]), -jnp.inf)
            probs = jnp.exp(scores - lse_ref[:, h : h + 1])
            grad_probs = contract_cols(grad_out, kv_all[:, HEAD:])
            delta = jnp.sum(probs * grad_probs, -1, keepdims=True)
            grad_scores = (probs * (grad_probs - delta)).astype(BF)
            ds_all[below, :] = grad_scores
            probs_all[below, :] = probs.astype(BF)
            q_all[below, :] = query
            do_all[below, :] = grad_out
            grad_query = jnp.dot(grad_scores, kv_all[:, :HEAD], preferred_element_type=F32)
            grad_query = unrotate(grad_query, cos_ref[...], sin_ref[...]) * query_scale
            dq_ref[:, at] = grad_query.astype(BF)
        for ref, first, kind in ((own_ref, 0, F32), (other_ref, half, BF)):
            part = pl.ds(first, half)
            ref[:, :HEAD] = contract_rows(ds_all[:, part], q_all[...]).astype(kind)
            ref[:, HEAD:] = contract_rows(probs_all[:, part], do_all[...]).astype(kind)

    stacked = HEADS * rows
    return pl.pallas_call(
        kernel,
        out_shape=(
            jax.ShapeDtypeStruct((rows, HEADS * HEAD), BF),
            jax.ShapeDtypeStruct((half, 2 * HEAD), F32),
            jax.ShapeDtypeStruct((half, 2 * HEAD), BF),
        ),
        scratch_shapes=[
            pltpu.VMEM((length, 2 * HEAD), BF),
            pltpu.VMEM((stacked, length), BF),
            pltpu.VMEM((stacked, length), BF),
            pltpu.VMEM((stacked, HEAD), BF),
            pltpu.VMEM((stacked, HEAD), BF),
        ],
        cost_estimate=pl.CostEstimate(
            flops=10 * rows * length * HEADS * HEAD,
            transcendentals=rows * length * HEADS,
            bytes_accessed=7 * length * HEAD + 10 * rows * HEADS * HEAD,
        ),
        name="attend_back",
    )(*kv_pieces, queries, cosine, sine_part, query_pos, key_pos, totals, grad_mixed)


def plane_specs(dp_count, rows_here):
    together = 2
    steps = dp_count // together

    def tokens(columns):
        return pl.BlockSpec(
            (together, 1, rows_here, columns),
            lambda i, core: (i % steps, jnp.where(i < steps, 1 - core[0], core[0]), 0, 0),
        )

    def halves(columns):
        rows = together * rows_here
        return (
            pl.BlockSpec((rows, columns), lambda i, core: (jnp.minimum(i, steps - 1), 0)),
            pl.BlockSpec((rows, columns), lambda i, core: (jnp.maximum(i - steps, 0), 0)),
        )

    return steps, together * rows_here, tokens, halves


def feed_forward(core, tokens_in, weight, grad_hidden):
    dp_count, _, rows_here, width = tokens_in.shape
    part = grad_hidden.shape[3]
    steps, rows, tokens, halves = plane_specs(dp_count, rows_here)

    def kernel(core_ref, in_ref, weight_ref, grad_ref, hid_ref, dgu_ref, other_ref, own_ref):
        step = pl.program_id(0)
        both = jnp.dot(in_ref[...].reshape(rows, width), weight_ref[...], preferred_element_type=F32)
        gelu_value, gelu_slope = gelu_parts(both[:, :part])
        up_part = both[:, part:]
        grad = grad_ref[...].reshape(rows, part)
        hid_ref[...] = (gelu_value * up_part).astype(BF).reshape(hid_ref.shape)
        dgu = jnp.concatenate([grad * up_part * gelu_slope, grad * gelu_value], 1).astype(BF)
        dgu_ref[...] = dgu.reshape(dgu_ref.shape)
        term = contract_cols(dgu, weight_ref[...]).astype(BF)

        @pl.when(step < steps)
        def _():
            other_ref[...] = term

        @pl.when(step >= steps)
        def _():
            own_ref[...] = term

    count = dp_count * CORES * rows_here
    half = jax.ShapeDtypeStruct((count // 2, width), BF)
    return pl.pallas_call(
        kernel,
        grid_spec=pltpu.PrefetchScalarGridSpec(
            num_scalar_prefetch=1,
            grid=(2 * steps,),
            in_specs=[
                tokens(width),
                pl.BlockSpec((width, 2 * part), lambda i, core: (0, 0)),
                tokens(part),
            ],
            out_specs=(tokens(part), tokens(2 * part), *halves(width)),
        ),
        out_shape=(
            jax.ShapeDtypeStruct((dp_count, CORES, rows_here, part), BF),
            jax.ShapeDtypeStruct((dp_count, CORES, rows_here, 2 * part), BF),
            half,
            half,
        ),
        cost_estimate=pl.CostEstimate(
            flops=8 * count * width * part,
            transcendentals=count * part,
            bytes_accessed=4 * count * width + 4 * width * part + 10 * count * part,
        ),
        name="feed_forward",
    )(core, tokens_in, weight, grad_hidden)


def row_product(left, right):
    tokens, width = left.shape
    columns = right.shape[1]
    block = 256 if tokens % 256 == 0 else tokens

    def kernel(left_ref, right_ref, out_ref):
        out_ref[...] = jnp.dot(left_ref[...], right_ref[...], preferred_element_type=F32)

    return pl.pallas_call(
        kernel,
        grid=(tokens // block,),
        in_specs=[
            pl.BlockSpec((block, width), lambda i: (i, 0)),
            pl.BlockSpec((width, columns), lambda i: (0, 0)),
        ],
        out_specs=pl.BlockSpec((block, columns), lambda i: (i, 0)),
        out_shape=jax.ShapeDtypeStruct((tokens, columns), F32),
        cost_estimate=pl.CostEstimate(
            flops=2 * tokens * width * columns,
            transcendentals=0,
            bytes_accessed=2 * (tokens * width + width * columns) + 4 * tokens * columns,
        ),
        name="row_product",
    )(left, right)


def key_value_grads(own, arrived, cosine, sine_part):
    rows, columns = arrived[0].shape

    def kernel(own_ref, cos_ref, sin_ref, *refs):
        total = own_ref[...]
        for ref in refs[:-1]:
            total = total + ref[...].astype(F32)
        grad_key = unrotate(total[:, :HEAD], cos_ref[...], sin_ref[...])
        refs[-1][...] = jnp.concatenate([grad_key, total[:, HEAD:]], 1).astype(BF)

    return pl.pallas_call(
        kernel, out_shape=jax.ShapeDtypeStruct((rows, columns), BF), name="key_value_grads"
    )(own, cosine, sine_part, *arrived)


def input_grads(grad_query, grad_kv, weight, grad_h, tokens, inverse, gain, counts):
    rows, width_q = grad_query.shape
    width = tokens.shape[1]
    dp_count, z_count = counts
    owned = width // (dp_count * CORES * z_count)

    def kernel(dq_ref, dkv_ref, weight_ref, grad_ref, token_ref, inv_ref, gain_ref, out_ref, row_ref):
        last = width_q + grad_kv.shape[1]
        grad = contract_cols(dq_ref[...], weight_ref[:, :width_q])
        grad = grad + contract_cols(dkv_ref[...], weight_ref[:, width_q:last])
        token = token_ref[...].astype(F32)
        inverse = inv_ref[...]
        scaled = gain_ref[...] * grad
        mean = jnp.mean(scaled * token, -1, keepdims=True)
        row_ref[...] = grad_ref[...] + inverse * scaled - token * inverse**3 * mean
        for d in range(dp_count):
            for c in range(CORES):
                for z in range(z_count):
                    source = pl.ds(((d * CORES + c) * z_count + z) * owned, owned)
                    target = pl.ds(((d * z_count + z) * CORES + c) * owned, owned)
                    out_ref[:, target] = row_ref[:, source]

    return pl.pallas_call(
        kernel,
        out_shape=jax.ShapeDtypeStruct((rows, width), F32),
        scratch_shapes=[pltpu.VMEM((rows, width), F32)],
        cost_estimate=pl.CostEstimate(
            flops=2 * rows * width * (width_q + grad_kv.shape[1]),
            transcendentals=0,
            bytes_accessed=2 * width * weight.shape[1] + 10 * rows * width,
        ),
        name="input_grads",
    )(grad_query, grad_kv, weight, grad_h, tokens, inverse, gain)


def down_product(core, hidden, weight):
    dp_count, _, rows_here, part = hidden.shape
    width = weight.shape[0]
    steps, rows, tokens, halves = plane_specs(dp_count, rows_here)

    def kernel(core_ref, in_ref, weight_ref, other_ref, own_ref):
        step = pl.program_id(0)
        term = contract_cols(in_ref[...].reshape(rows, part), weight_ref[...]).astype(BF)

        @pl.when(step < steps)
        def _():
            other_ref[...] = term

        @pl.when(step >= steps)
        def _():
            own_ref[...] = term

    count = dp_count * CORES * rows_here
    half = jax.ShapeDtypeStruct((count // 2, width), BF)
    return pl.pallas_call(
        kernel,
        grid_spec=pltpu.PrefetchScalarGridSpec(
            num_scalar_prefetch=1,
            grid=(2 * steps,),
            in_specs=[tokens(part), pl.BlockSpec((width, part), lambda i, core: (0, 0))],
            out_specs=halves(width),
        ),
        out_shape=(half, half),
        cost_estimate=pl.CostEstimate(
            flops=2 * count * width * part,
            transcendentals=0,
            bytes_accessed=2 * count * (width + part) + 2 * width * part,
        ),
        name="down_product",
    )(core, hidden, weight)


def weight_term(left, right, dp_count, z_count):
    tokens, width = left.shape
    columns = right.shape[1]
    per_dp = width // dp_count
    owned = per_dp // (z_count * CORES)
    together = 1
    while (together * per_dp) % LANES:
        together *= 2
    block = together * per_dp

    def kernel(left_ref, right_ref, out_ref):
        term = contract_rows(left_ref[...], right_ref[...]).astype(BF)
        for d in range(together):
            for c in range(CORES):
                for z in range(z_count):
                    first = d * per_dp + (c * z_count + z) * owned
                    out_ref[z, d, c] = term[first : first + owned]

    return pl.pallas_call(
        kernel,
        grid=(width // block,),
        in_specs=[
            pl.BlockSpec((tokens, block), lambda i: (0, i)),
            pl.BlockSpec((tokens, columns), lambda i: (0, 0)),
        ],
        out_specs=pl.BlockSpec(
            (z_count, together, CORES, owned, columns), lambda i: (0, i, 0, 0, 0)
        ),
        out_shape=jax.ShapeDtypeStruct((z_count, dp_count, CORES, owned, columns), BF),
        cost_estimate=pl.CostEstimate(
            flops=2 * tokens * width * columns,
            transcendentals=0,
            bytes_accessed=2 * (tokens * width + tokens * columns + width * columns),
        ),
        name="weight_term",
    )(left, right)


def body(
    block_input, qkv_weight, out_weight, ffn_weight, down_weight, attn_gain, ffn_gain, cotangent
):
    tokens = block_input[0]
    cot_rows = cotangent[0]
    rows_here, width = tokens.shape
    owned_rows = qkv_weight.shape[0]
    dp_count = lax.axis_size("da") * lax.axis_size("db")
    z_count = lax.axis_size("z")
    z_index = lax.axis_index("z")
    core = lax.axis_index("core")
    group = dp_count * CORES
    width_q = HEADS * HEAD
    width_qkv = width_q + 2 * HEAD
    part = -(-FF // (LANES * group)) * LANES

    tokens = reorder(tokens, dp_count, z_count, CORES)
    cot_rows = reorder(cot_rows, dp_count, z_count, CORES)

    gain_columns = jnp.stack([attn_gain, ffn_gain], 1)
    gain_columns = jnp.pad(gain_columns, ((0, 0), (0, LANES - 2)))
    qkv_line = gather(jnp.concatenate([qkv_weight, gain_columns], 1), "z")
    packed = pack_shares(ffn_weight, down_weight, group, part)
    mine = exchange(packed, PLANE)
    qkv_line, mine, out_weight = lax.optimization_barrier((qkv_line, mine, out_weight))
    down_mine, gate_up_mine = mine[..., 2 * part :], mine[..., : 2 * part]
    down_lines = line_gather(down_mine, "z")
    gate_up_lines = line_gather(gate_up_mine, "z")
    down_w = place_line(z_index, z_count, down_mine, *down_lines)
    gate_up_w = place_line(z_index, z_count, gate_up_mine, *gate_up_lines)
    qkv_gain = gather(qkv_line, PLANE)
    qkv_full = qkv_gain[:, :width_qkv]
    gain_one = qkv_gain[:, width_qkv].astype(F32)
    gain_two = qkv_gain[:, width_qkv + 1].astype(F32)
    out_pieces = [out_weight] + [shift(out_weight, "z", k) for k in range(1, z_count)]
    out_places = [behind(z_index, k, z_count) for k in range(z_count)]
    out_pieces = [(0, piece) for piece in out_pieces]
    out_line = gather_blocks(out_pieces, out_places, owned_rows, z_count)
    out_line = out_line.reshape(z_count * owned_rows, width_q)
    out_full = plane_gather(out_line, False)
    cot_plane = plane_gather(cot_rows, True)

    positions = (z_index * CORES + core) * rows_here + jnp.arange(rows_here, dtype=jnp.int32)
    cosine, sine_part = rope_tables(positions)
    token_f = tokens.astype(jnp.float32)
    inv_one = lax.rsqrt(jnp.mean(token_f * token_f, -1, keepdims=True) + EPSILON)
    normed_one = (token_f * inv_one * gain_one).astype(jnp.bfloat16)
    qkv_rows = jnp.dot(normed_one, qkv_full, preferred_element_type=jnp.float32)
    keys_own = rotate(qkv_rows[:, width_q : width_q + HEAD], cosine, sine_part).astype(jnp.bfloat16)
    kv_rows = jnp.concatenate([keys_own, qkv_rows[:, width_q + HEAD :].astype(jnp.bfloat16)], -1)
    kv_pieces = [kv_rows] + [shift(kv_rows, "z", k) for k in range(1, z_count)]
    kv_pieces = kv_pieces + [shift(piece, "core", 1) for piece in kv_pieces]
    block_z = lax.rem(z_index + z_count - jnp.arange(z_count, dtype=jnp.int32), z_count)
    block_at = jnp.concatenate([block_z * CORES + core, block_z * CORES + (1 - core)])
    key_pos = (
        block_at[:, None] * rows_here + jnp.arange(rows_here, dtype=jnp.int32)[None, :]
    ).reshape(1, -1)
    query_pos = positions[:, None]
    attn_flat, log_total, queries = attend(
        qkv_rows, kv_pieces, cosine, sine_part, query_pos, key_pos
    )
    hidden_one = token_f + contract_cols(attn_flat, out_full)
    inv_two = lax.rsqrt(jnp.mean(hidden_one * hidden_one, -1, keepdims=True) + EPSILON)
    normed_two = (hidden_one * inv_two * gain_two).astype(jnp.bfloat16)

    normed_plane = gather(normed_two, PLANE)
    grad_hidden = row_product(cot_plane, down_w)
    core_at = jnp.full((1,), core, jnp.int32)
    at = jnp.stack([lax.axis_index(axis) for axis in ("da", "db", "core", "z")]).astype(jnp.int32)
    in_blocks = (dp_count, CORES, rows_here, -1)
    hidden, grad_gate_up, dn2_other, dn2_own = feed_forward(
        core_at, normed_plane.reshape(in_blocks), gate_up_w, grad_hidden.reshape(in_blocks)
    )
    dn2_halves = reduce_tokens(dn2_own, dn2_other, None)
    down_other, down_own = down_product(core_at, hidden, down_w)
    down_halves = reduce_tokens(down_own, down_other, at)
    output_rows = reorder(hidden_one, dp_count, CORES, z_count, down_halves, BF)

    def sum_ffn(left, right):
        right = right.reshape(left.shape[0], -1)
        term = weight_term(left, right, dp_count, z_count).reshape(width, right.shape[1])
        return scatter(term, "z").reshape(group, owned_rows, right.shape[1])

    gate_up_sum = sum_ffn(normed_plane, grad_gate_up)
    gate_up_sum = exchange(gate_up_sum, PLANE)
    down_sum = sum_ffn(cot_plane, hidden)
    down_sum, gate_up_sum = lax.optimization_barrier((down_sum, gate_up_sum))
    down_sum = exchange(down_sum, PLANE)
    grad_ffn, gain_two_grad = unpack_gate_up(gate_up_sum, ffn_weight, ffn_gain, group, part)
    gain_two_grad = gain_two_grad[:, 0]
    grad_down = unpack_down(down_sum, FF, group, part)

    grad_h_one, grad_h_bf = hidden_grads(dn2_halves, cot_rows, hidden_one, inv_two, gain_two[None])
    grad_attn = jnp.dot(grad_h_bf, out_full, preferred_element_type=F32).astype(BF)
    grad_query, kv_own, kv_other = attend_back(
        queries, kv_pieces, cosine, sine_part, query_pos, key_pos, log_total, grad_attn
    )
    kv_other = shift(kv_other, "core", 1)
    paired = (kv_own + kv_other.astype(F32)).reshape(z_count, rows_here, 2 * HEAD)
    arrived = []
    for k in range(1, z_count):
        piece = paired[k].astype(BF)
        arrived.append(shift(piece, "z", -k))
    grad_kv = key_value_grads(paired[0], arrived, cosine, sine_part)

    grad_rows = input_grads(
        grad_query, grad_kv, qkv_gain, grad_h_one, tokens, inv_one, gain_one[None], (dp_count, z_count)
    )

    out_halves = reduce_term(grad_h_bf, attn_flat, at)
    query_halves = reduce_term(normed_one, grad_query, None)
    kv_halves = reduce_term(normed_one, grad_kv, None)
    terms = reduce_line([out_halves, query_halves, kv_halves], at, owned_rows)
    grad_out, grad_qkv, gain_one_grad = attention_weight_grads(terms, qkv_weight, attn_gain)
    gain_one_grad = gain_one_grad[:, 0]
    return (
        output_rows[None],
        grad_rows[None],
        grad_qkv,
        grad_out,
        grad_ffn,
        grad_down,
        gain_one_grad,
        gain_two_grad,
    )


def solution(mesh):
    dp_count = mesh.shape["dp"]
    seq_count = mesh.shape["seq"]
    split = Mesh(mesh.devices.reshape(dp_count // 2, 2, seq_count // CORES, CORES), EVERY)
    by_token = P(PAIR, SEQ, None)
    by_row = P(EVERY, None)
    by_gain = P(EVERY)


    return jax.shard_map(
        body,
        mesh=split,
        in_specs=(by_token, by_row, by_row, by_row, by_row, by_gain, by_gain, by_token),
        out_specs=(by_token, by_token, by_row, by_row, by_row, by_row, by_gain, by_gain),
        check_vma=False,
    )
```
